32 devices in a mesh: gx: 8 (over y, x, core), gy: 4 (over z).
Axes of the slice: x: 2, y: 2, z: 4, core: 2. Of those that a mesh axis runs over, the one named last changes fastest.
Arguments:
- velocity: float32 [128, 64, 3, 16], P('gx', 'gy'), may hold values from -6 to 6
- x_sizes: float32 [16], P('gx'), may hold values from 0.5 to 2
- y_sizes: float32 [8], P('gy'), may hold values from 0.5 to 2
- z_sizes: float32 [2], replicated, may hold values from 0.25 to 2
- layer_counts: int32 [8, 4], P('gx', 'gy'), may hold values from 1 to 2, as said below
Outputs:
- advected: float32 [128, 64, 3, 16], P('gx', 'gy')
- pressure: float32 [128, 64, 16], P('gx', 'gy')
The draws below stay inside these ranges and needn't reach their ends.
Inputs may be any that keep to these rules, and one draw needn't show every extreme that they name: `layer_counts`: counted from the lower wall; layers at and above the count hold no element. Some device holds all 2 layers.
All inputs are finite; a program needn't handle non-finite values.
Results may differ from the reference program's by a relative error of at most 0.0003.
Values sent between devices are 32-bit elements; how exact they have to be, the bound alone decides.
A program may use at most 64 MiB of HBM per device.

```python
import math
import jax
import jax.numpy as jnp
from jax import lax

EX = 2
EY = 2
EZ = 2
SWEEPS = 2
NEX = 16
NEY = 8
NXN = 128
NYN = 64
NZN = 16
N_GX = 8
N_GY = 4


def draw_layer_counts(key, part):
    key_counts, key_spot = jax.random.split(jax.random.fold_in(key, 17))
    counts = jax.random.randint(key_counts, (N_GX * N_GY,), EZ // 2, EZ + 1)
    full_spot = jax.random.randint(key_spot, (), 0, N_GX * N_GY)
    flat_counts = jnp.where(jnp.arange(N_GX * N_GY) == full_spot, EZ, counts)
    return flat_counts.reshape(N_GX, N_GY).astype(jnp.int32)


def steps_of(key, shape, shards, low, high):
    def one(position, blocks):
        draws = jax.random.uniform(jax.random.fold_in(jax.random.fold_in(key, 6), position), (blocks,), jnp.float32, low / len(shards), high / len(shards))
        return jnp.repeat(jnp.exp(draws), shape[position] // blocks).reshape((-1,) + (1,) * (len(shape) - position - 1))

    gain = one(*shards[0])
    for cut in shards[1:]:
        gain = gain * one(*cut)
    return gain


def noise(key, dims, deviation, limit, shards=(), held_as=jnp.bfloat16):
    values = jax.random.normal(key, dims, jnp.float32) * deviation
    if len(shards) > 0:
        values = steps_of(key, dims, shards, -0.22, 0.18) * values
    return jnp.clip(values, min=-limit, max=limit).astype(held_as)


def setup_inputs(seed: int = 0) -> dict:
    arg_keys = jax.random.split(jax.random.key(seed), 6)
    return {
        "velocity": noise(arg_keys[0], (NXN, NYN, 3, NZN), 1.0, 6.0, ((0, 8), (1, 4)), jnp.float32),
        "x_sizes": jnp.clip(jnp.exp(math.log(2.0) - 1.3862944 * jax.random.uniform(arg_keys[1], (NEX,), jnp.float32) ** steps_of(arg_keys[1], (NEX,), ((0, 8),), -0.2, 0.2)), 0.5, 2.0),
        "y_sizes": jnp.clip(jnp.exp(math.log(2.0) - 1.3862944 * jax.random.uniform(arg_keys[2], (NEY,), jnp.float32) ** steps_of(arg_keys[2], (NEY,), ((0, 4),), -0.2, 0.2)), 0.5, 2.0),
        "z_sizes": jnp.clip(jnp.exp(jax.random.uniform(arg_keys[3], (EZ,), jnp.float32, math.log(0.25), math.log(2.0))), 0.25, 2.0),
        "layer_counts": draw_layer_counts(jax.random.fold_in(arg_keys[5], 71), 0),
    }


HIGHEST = lax.Precision.HIGHEST
time_step = 0.005

def legendre_value(order, point):
    previous = 1.0
    current = point
    for degree in range(2, order + 1):
        previous, current = (current, ((2 * degree - 1) * point * current - (degree - 1) * previous) / degree)
    return current

def legendre_pair(order, point):
    previous = 1.0
    current = point
    for degree in range(2, order + 1):
        previous, current = (current, ((2 * degree - 1) * point * current - (degree - 1) * previous) / degree)
    slope = order * (point * current - previous) / (point * point - 1.0)
    return (current, slope)

def tables():
    inner_points = []
    for index in range(1, 7):
        point = -math.cos(math.pi * index / 7.0)
        for newton in range(60):
            value, slope = legendre_pair(7, point)
            curvature = (2.0 * point * slope - 56.0 * value) / (1.0 - point * point)
            point = point - slope / curvature
        inner_points.append(point)
    gll_points = [-1.0] + inner_points + [1.0]
    gll_weights = [2.0 / (56.0 * legendre_value(7, point) ** 2) for point in gll_points]
    barycentric = []
    for first in range(8):
        product = 1.0
        for second in range(8):
            if second != first:
                product = product * (gll_points[first] - gll_points[second])
        barycentric.append(1.0 / product)
    derivative = [[0.0] * 8 for first in range(8)]
    for first in range(8):
        total = 0.0
        for second in range(8):
            if second != first:
                entry = barycentric[second] / barycentric[first] / (gll_points[first] - gll_points[second])
                derivative[first][second] = entry
                total = total + entry
        derivative[first][first] = -total
    gauss_points = []
    gauss_weights = []
    for index in range(1, 13):
        point = -math.cos(math.pi * (index - 0.25) / 12.5)
        for newton in range(60):
            value, slope = legendre_pair(12, point)
            point = point - value / slope
        value, slope = legendre_pair(12, point)
        gauss_points.append(point)
        gauss_weights.append(2.0 / ((1.0 - point * point) * slope * slope))
    interpolate = []
    for gauss in gauss_points:
        fraction = [barycentric[node] / (gauss - gll_points[node]) for node in range(8)]
        total = sum(fraction)
        interpolate.append([entry / total for entry in fraction])
    stiffness = [[sum((derivative[inner][first] * gll_weights[inner] * derivative[inner][second] for inner in range(8))) for second in range(8)] for first in range(8)]
    glob_stiff = [[0.0] * 22 for first in range(22)]
    glob_mass = [0.0] * 22
    for offset in (0, 7, 14):
        for first in range(8):
            glob_mass[offset + first] = glob_mass[offset + first] + gll_weights[first]
            for second in range(8):
                glob_stiff[offset + first][offset + second] = glob_stiff[offset + first][offset + second] + stiffness[first][second]
    inv_root = [1.0 / math.sqrt(glob_mass[6 + first]) for first in range(10)]
    matrix = [[inv_root[first] * glob_stiff[6 + first][6 + second] * inv_root[second] for second in range(10)] for first in range(10)]
    rotation = [[1.0 if first == second else 0.0 for second in range(10)] for first in range(10)]
    for sweep in range(20):
        for first in range(10):
            for second in range(first + 1, 10):
                angle = 0.5 * math.atan2(2.0 * matrix[first][second], matrix[second][second] - matrix[first][first])
                cosine = math.cos(angle)
                sine = math.sin(angle)
                for other in range(10):
                    left_val = matrix[other][first]
                    right_val = matrix[other][second]
                    matrix[other][first] = cosine * left_val - sine * right_val
                    matrix[other][second] = sine * left_val + cosine * right_val
                    left_val = rotation[other][first]
                    right_val = rotation[other][second]
                    rotation[other][first] = cosine * left_val - sine * right_val
                    rotation[other][second] = sine * left_val + cosine * right_val
                for other in range(10):
                    upper_val = matrix[first][other]
                    lower_val = matrix[second][other]
                    matrix[first][other] = cosine * upper_val - sine * lower_val
                    matrix[second][other] = sine * upper_val + cosine * lower_val
    eigen_values = [matrix[first][first] for first in range(10)]
    vectors = [[inv_root[first] * rotation[first][second] for second in range(10)] for first in range(10)]
    return tuple((jnp.asarray(table, dtype=jnp.float32) for table in (derivative, gll_weights, interpolate, gauss_weights, stiffness, vectors, eigen_values)))

def along_x(matrix, values):
    return jnp.einsum('mi,aibjczk->ambjczk', matrix, values, precision=HIGHEST)

def along_y(matrix, values):
    return jnp.einsum('mj,aibjczk->aibmczk', matrix, values, precision=HIGHEST)

def along_z(matrix, values):
    return jnp.einsum('mk,aibjczk->aibjczm', matrix, values, precision=HIGHEST)

def shaped(x_len, y_len, z_len):
    return (x_len.reshape(-1, 1, 1, 1, 1, 1, 1), y_len.reshape(1, 1, -1, 1, 1, 1, 1), z_len.reshape(1, 1, 1, 1, 1, -1, 1))

def node_weights(gll_weights):
    return (gll_weights.reshape(1, 8, 1, 1, 1, 1, 1), gll_weights.reshape(1, 1, 1, 8, 1, 1, 1), gll_weights.reshape(1, 1, 1, 1, 1, 1, 8))

def advection_terms(vel_el, x_len, y_len, z_len, active, tabs):
    derivative, gll_weights, interpolate, gauss_weights, stiffness, vectors, eigen = tabs
    hx_b, hy_b, hz_b = shaped(x_len, y_len, z_len)
    inter_d = jnp.dot(interpolate, derivative, precision=HIGHEST)
    zpass = along_z(interpolate, vel_el)
    zypass = along_y(interpolate, zpass)
    at_gauss = along_x(interpolate, zypass)
    grad_x = along_x(inter_d, zypass) * (2.0 / hx_b)
    grad_y = along_x(interpolate, along_y(inter_d, zpass)) * (2.0 / hy_b)
    grad_z = along_x(interpolate, along_y(interpolate, along_z(inter_d, vel_el))) * (2.0 / hz_b)
    convect = at_gauss[:, :, :, :, 0:1] * grad_x + at_gauss[:, :, :, :, 1:2] * grad_y + at_gauss[:, :, :, :, 2:3] * grad_z
    jacobian = hx_b * hy_b * hz_b / 8.0
    quadrature = gauss_weights.reshape(1, 12, 1, 1, 1, 1, 1) * gauss_weights.reshape(1, 1, 1, 12, 1, 1, 1) * gauss_weights.reshape(1, 1, 1, 1, 1, 1, 12)
    back = interpolate.T
    weak = along_x(back, along_y(back, along_z(back, convect * quadrature * jacobian)))
    w_i, w_j, w_k = node_weights(gll_weights)
    mass = jacobian * w_i * w_j * w_k
    active_full = jnp.broadcast_to(active, mass.shape)
    return jnp.concatenate([weak * active, mass * active, active_full], axis=4)

def divergence_terms(adv_el, x_len, y_len, z_len, active, tabs):
    derivative, gll_weights = (tabs[0], tabs[1])
    hx_b, hy_b, hz_b = shaped(x_len, y_len, z_len)
    diverge = along_x(derivative, adv_el[:, :, :, :, 0:1]) * (2.0 / hx_b)
    diverge = diverge + along_y(derivative, adv_el[:, :, :, :, 1:2]) * (2.0 / hy_b)
    diverge = diverge + along_z(derivative, adv_el[:, :, :, :, 2:3]) * (2.0 / hz_b)
    w_i, w_j, w_k = node_weights(gll_weights)
    mass = hx_b * hy_b * hz_b / 8.0 * w_i * w_j * w_k
    return -mass * diverge * active

def laplacian(press_el, x_len, y_len, z_len, active, tabs):
    gll_weights, stiffness = (tabs[1], tabs[4])
    hx_b, hy_b, hz_b = shaped(x_len, y_len, z_len)
    w_i, w_j, w_k = node_weights(gll_weights)
    result = hy_b * hz_b / (2.0 * hx_b) * along_x(stiffness, press_el) * w_j * w_k
    result = result + hx_b * hz_b / (2.0 * hy_b) * along_y(stiffness, press_el) * w_i * w_k
    result = result + hx_b * hy_b / (2.0 * hz_b) * along_z(stiffness, press_el) * w_i * w_j
    return result * active

def schwarz_solve(extended, x_len, y_len, z_len, active, tabs):
    vectors, eigen = (tabs[5], tabs[6])
    hx_b, hy_b, hz_b = shaped(x_len, y_len, z_len)
    forward = vectors.T
    spectral = along_x(forward, along_y(forward, along_z(forward, extended)))
    denom = hy_b * hz_b / (2.0 * hx_b) * eigen.reshape(1, 10, 1, 1, 1, 1, 1)
    denom = denom + hx_b * hz_b / (2.0 * hy_b) * eigen.reshape(1, 1, 1, 10, 1, 1, 1)
    denom = denom + hx_b * hy_b / (2.0 * hz_b) * eigen.reshape(1, 1, 1, 1, 1, 1, 10)
    solved = along_x(vectors, along_y(vectors, along_z(vectors, spectral / denom)))
    return solved[:, 1:9, :, 1:9, :, :, 1:9] * active

def pair_sum(padded, which_axis, elem_count):
    pair_sums = lax.slice_in_dim(padded, 0, 8 * elem_count + 1, stride=8, axis=which_axis) + lax.slice_in_dim(padded, 1, 8 * elem_count + 2, stride=8, axis=which_axis)
    interior = lax.slice_in_dim(padded, 1, 8 * elem_count + 1, axis=which_axis)
    dims_before = interior.shape[:which_axis]
    dims_after = interior.shape[which_axis + 1:]
    element_grid = interior.reshape(dims_before + (elem_count, 8) + dims_after)
    lower_face = lax.slice_in_dim(pair_sums, 0, elem_count, axis=which_axis).reshape(dims_before + (elem_count, 1) + dims_after)
    upper_face = lax.slice_in_dim(pair_sums, 1, elem_count + 1, axis=which_axis).reshape(dims_before + (elem_count, 1) + dims_after)
    inner_planes = lax.slice_in_dim(element_grid, 1, 7, axis=which_axis + 1)
    joined = jnp.concatenate([lower_face, inner_planes, upper_face], axis=which_axis + 1)
    return joined.reshape(interior.shape)

def pair_z(nodal, ez_count):
    element_grid = nodal.reshape(nodal.shape[:-1] + (ez_count, 8))
    pair_sums = element_grid[..., :-1, 7] + element_grid[..., 1:, 0]
    first_plane = jnp.concatenate([element_grid[..., 0:1, 0], pair_sums], axis=-1)
    last_plane = jnp.concatenate([pair_sums, element_grid[..., -1:, 7]], axis=-1)
    joined = jnp.concatenate([first_plane[..., None], element_grid[..., 1:7], last_plane[..., None]], axis=-1)
    return joined.reshape(nodal.shape)

def extend_axis(padded, which_axis, elem_count):
    dims_before = padded.shape[:which_axis]
    dims_after = padded.shape[which_axis + 1:]
    lower_rim = lax.slice_in_dim(padded, 0, 8 * elem_count - 7, stride=8, axis=which_axis).reshape(dims_before + (elem_count, 1) + dims_after)
    upper_rim = lax.slice_in_dim(padded, 11, 8 * elem_count + 4, stride=8, axis=which_axis).reshape(dims_before + (elem_count, 1) + dims_after)
    middle = lax.slice_in_dim(padded, 2, 2 + 8 * elem_count, axis=which_axis).reshape(dims_before + (elem_count, 8) + dims_after)
    return jnp.concatenate([lower_rim, middle, upper_rim], axis=which_axis + 1)

def by_slabs(func, arrays, x_len, active):
    groups = x_len.shape[0] // EX

    def to_groups(array):
        return array.reshape((groups, array.shape[0] // groups) + array.shape[1:])

    def per_group(members):
        pieces, x_piece, act_piece = members
        return func(pieces, x_piece, act_piece)
    result = lax.map(per_group, (tuple((to_groups(array) for array in arrays)), to_groups(x_len), to_groups(active)))
    return result.reshape((result.shape[0] * result.shape[1],) + result.shape[2:])

def assemble(nodal, ex_total, ey_total):
    padded = jnp.pad(nodal, ((1, 1), (1, 1), (0, 0), (0, 0)), mode='wrap')
    return pair_z(pair_sum(pair_sum(padded, 0, ex_total), 1, ey_total), EZ)

def reference(velocity, x_sizes, y_sizes, z_sizes, layer_counts):
    tabs = tables()
    ex_total = x_sizes.shape[0]
    ey_total = y_sizes.shape[0]
    repeated = jnp.repeat(jnp.repeat(layer_counts, EX, axis=0), EY, axis=1)
    layers = jnp.arange(EZ).astype(jnp.int32)
    active = (layers[None, None, :] < repeated[:, :, None]).astype(jnp.float32).reshape(ex_total, 1, ey_total, 1, 1, EZ, 1)
    node_shape = (8 * ex_total, 8 * ey_total)
    vel_el = velocity.reshape(ex_total, 8, ey_total, 8, 3, EZ, 8)
    stacked = by_slabs(lambda pieces, x_piece, act_piece: advection_terms(pieces[0], x_piece, y_sizes, z_sizes, act_piece, tabs), (vel_el,), x_sizes, active)
    sums = assemble(stacked.reshape(node_shape + (5, 8 * EZ)), ex_total, ey_total)
    mult = sums[:, :, 4:5]
    convection = sums[:, :, 0:3] / jnp.where(mult > 0.5, sums[:, :, 3:4], 1.0)
    advected_el = (vel_el - time_step * convection.reshape(vel_el.shape)) * active
    rhs_el = by_slabs(lambda pieces, x_piece, act_piece: divergence_terms(pieces[0], x_piece, y_sizes, z_sizes, act_piece, tabs), (advected_el,), x_sizes, active)
    rhs = assemble(rhs_el.reshape(node_shape + (1, 8 * EZ)), ex_total, ey_total)
    press_el = jnp.zeros((ex_total, 8, ey_total, 8, 1, EZ, 8), jnp.float32)
    for sweep_index in range(SWEEPS):
        if sweep_index == 0:
            residual = rhs
        else:
            applied = by_slabs(lambda pieces, x_piece, act_piece: laplacian(pieces[0], x_piece, y_sizes, z_sizes, act_piece, tabs), (press_el,), x_sizes, active)
            residual = rhs - assemble(applied.reshape(residual.shape), ex_total, ey_total)
        padded = jnp.pad(residual, ((2, 2), (2, 2), (0, 0), (0, 0)), mode='wrap')
        padded = jnp.pad(padded, ((0, 0), (0, 0), (0, 0), (2, 2)))
        extended = extend_axis(extend_axis(extend_axis(padded, 0, ex_total), 2, ey_total), 5, EZ)
        local_fix = by_slabs(lambda pieces, x_piece, act_piece: schwarz_solve(pieces[0], x_piece, y_sizes, z_sizes, act_piece, tabs), (extended,), x_sizes, active)
        correction = assemble(local_fix.reshape(residual.shape), ex_total, ey_total) / jnp.maximum(mult, 1.0)
        press_el = press_el + correction.reshape(press_el.shape) * active
    advected = advected_el.reshape(node_shape + (3, 8 * EZ))
    pressure = press_el.reshape(node_shape + (8 * EZ,))
    return (advected, pressure)
```

```python
import functools
import math

import jax
import jax.numpy as jnp
import numpy as np
from jax import lax
from jax.experimental import pallas as pl
from jax.experimental.pallas import tpu as pltpu
from jax.sharding import PartitionSpec as P

SWEEPS = 2
time_step = 0.005
MESH = pl.DeviceIdType.MESH
F32 = jnp.float32
BF16 = jnp.bfloat16


def legendre_value(order, point):
    previous = 1.0
    current = point
    for degree in range(2, order + 1):
        previous, current = (
            current,
            ((2 * degree - 1) * point * current - (degree - 1) * previous) / degree,
        )
    return current


def legendre_pair(order, point):
    previous = 1.0
    current = point
    for degree in range(2, order + 1):
        previous, current = (
            current,
            ((2 * degree - 1) * point * current - (degree - 1) * previous) / degree,
        )
    slope = order * (point * current - previous) / (point * point - 1.0)
    return (current, slope)


def tables():
    inner_points = []
    for index in range(1, 7):
        point = -math.cos(math.pi * index / 7.0)
        for newton in range(60):
            value, slope = legendre_pair(7, point)
            curvature = (2.0 * point * slope - 56.0 * value) / (1.0 - point * point)
            point = point - slope / curvature
        inner_points.append(point)
    gll_points = [-1.0] + inner_points + [1.0]
    gll_weights = [2.0 / (56.0 * legendre_value(7, point) ** 2) for point in gll_points]
    barycentric = []
    for first in range(8):
        product = 1.0
        for second in range(8):
            if second != first:
                product = product * (gll_points[first] - gll_points[second])
        barycentric.append(1.0 / product)
    derivative = [[0.0] * 8 for first in range(8)]
    for first in range(8):
        total = 0.0
        for second in range(8):
            if second != first:
                entry = (
                    barycentric[second]
                    / barycentric[first]
                    / (gll_points[first] - gll_points[second])
                )
                derivative[first][second] = entry
                total = total + entry
        derivative[first][first] = -total
    gauss_points = []
    gauss_weights = []
    for index in range(1, 13):
        point = -math.cos(math.pi * (index - 0.25) / 12.5)
        for newton in range(60):
            value, slope = legendre_pair(12, point)
            point = point - value / slope
        value, slope = legendre_pair(12, point)
        gauss_points.append(point)
        gauss_weights.append(2.0 / ((1.0 - point * point) * slope * slope))
    interpolate = []
    for gauss in gauss_points:
        fraction = [barycentric[node] / (gauss - gll_points[node]) for node in range(8)]
        total = sum(fraction)
        interpolate.append([entry / total for entry in fraction])
    stiffness = [
        [
            sum(
                (
                    derivative[inner][first] * gll_weights[inner] * derivative[inner][second]
                    for inner in range(8)
                )
            )
            for second in range(8)
        ]
        for first in range(8)
    ]
    glob_stiff = [[0.0] * 22 for first in range(22)]
    glob_mass = [0.0] * 22
    for offset in (0, 7, 14):
        for first in range(8):
            glob_mass[offset + first] = glob_mass[offset + first] + gll_weights[first]
            for second in range(8):
                glob_stiff[offset + first][offset + second] = (
                    glob_stiff[offset + first][offset + second] + stiffness[first][second]
                )
    inv_root = [1.0 / math.sqrt(glob_mass[6 + first]) for first in range(10)]
    matrix = [
        [
            inv_root[first] * glob_stiff[6 + first][6 + second] * inv_root[second]
            for second in range(10)
        ]
        for first in range(10)
    ]
    rotation = [[1.0 if first == second else 0.0 for second in range(10)] for first in range(10)]
    for sweep in range(20):
        for first in range(10):
            for second in range(first + 1, 10):
                angle = 0.5 * math.atan2(
                    2.0 * matrix[first][second], matrix[second][second] - matrix[first][first]
                )
                cosine = math.cos(angle)
                sine = math.sin(angle)
                for other in range(10):
                    left_val = matrix[other][first]
                    right_val = matrix[other][second]
                    matrix[other][first] = cosine * left_val - sine * right_val
                    matrix[other][second] = sine * left_val + cosine * right_val
                    left_val = rotation[other][first]
                    right_val = rotation[other][second]
                    rotation[other][first] = cosine * left_val - sine * right_val
                    rotation[other][second] = sine * left_val + cosine * right_val
                for other in range(10):
                    upper_val = matrix[first][other]
                    lower_val = matrix[second][other]
                    matrix[first][other] = cosine * upper_val - sine * lower_val
                    matrix[second][other] = sine * upper_val + cosine * lower_val
    eigen_values = [matrix[first][first] for first in range(10)]
    vectors = [
        [inv_root[first] * rotation[first][second] for second in range(10)] for first in range(10)
    ]
    return tuple(
        np.asarray(table, dtype=np.float64)
        for table in (
            derivative,
            gll_weights,
            interpolate,
            gauss_weights,
            stiffness,
            vectors,
            eigen_values,
        )
    )


def halves(matrix):
    matrix = np.asarray(matrix, np.float32)
    high = matrix.astype(BF16)
    low = (matrix - high.astype(np.float32)).astype(BF16)
    return np.stack([high, low])


def padded(matrix, rows, cols, fill=0.0):
    out = np.full((rows, cols), fill, np.float64)
    out[: matrix.shape[0], : matrix.shape[1]] = matrix
    return out


def face_sum(count):
    out = np.eye(8 * count)
    for face in range(1, count):
        out[8 * face - 1, 8 * face] = 1.0
        out[8 * face, 8 * face - 1] = 1.0
    return out


def up8(value, step):
    return -(-value // step) * step


def constants(ex, ey, ez):
    deriv, gll, interp, gauss, stiff, vecs, lam = tables()
    eye = np.eye
    gx_rows = up8(12 * ex, 8)
    nz = 8 * ez
    tile = 8 * nz
    glanes = up8(144 * ez, 128)
    int_d = interp @ deriv
    sum_z = face_sum(ez)
    jx = padded(np.kron(eye(ex), interp), gx_rows, 8 * ex)
    dx = padded(np.kron(eye(ex), int_d), gx_rows, 8 * ex)
    l_in = np.concatenate([np.kron(eye(3), jx), np.kron(eye(3), dx)])
    jz = np.kron(eye(ez), interp)
    dz = np.kron(eye(ez), int_d)
    r_in = np.concatenate(
        [
            padded(np.kron(a, b).T, tile, glanes)
            for a, b in ((interp, jz), (int_d, jz), (interp, dz))
        ],
        axis=1,
    )
    r_back = padded(np.kron(interp, jz @ sum_z.T), glanes, tile)
    l_back = np.kron(eye(3), face_sum(ex) @ jx.T)
    ring_x = 8 * (ex + 2)
    l_div = np.kron(eye(ex + 2), deriv)
    l_lap = np.kron(eye(ex + 2), stiff)
    r_div_y = np.kron(deriv.T, eye(nz))
    r_div_z = np.kron(eye(8), np.kron(eye(ez), deriv.T))
    r_lap_y = np.kron(stiff.T, eye(nz))
    r_lap_z = np.kron(eye(8), np.kron(eye(ez), stiff.T))
    sx_rows = up8(10 * ex, 8)

    def extend(count):
        out = np.zeros((10 * count, 8 * (count + 2)))
        for elem in range(count):
            base = 8 * (elem + 1)
            out[10 * elem, base - 2] = 1.0
            for node in range(8):
                out[10 * elem + 1 + node, base + node] = 1.0
            out[10 * elem + 9, base + 9] = 1.0
        return out

    l_spec = padded(
        np.kron(eye(ex), vecs.T) @ extend(ex) @ face_sum(ex + 2), sx_rows, ring_x
    )
    ext_y = vecs.T @ extend(1) @ face_sum(3)
    ext_z = np.kron(eye(ez), vecs.T) @ extend(ez)[:, 8:-8] @ sum_z
    slanes = up8(100 * ez, 128)
    r_spec = padded(np.kron(ext_y, ext_z).T, 3 * tile, slanes)
    inner = vecs[1:9]
    r_fix = padded(np.kron(inner, sum_z @ np.kron(eye(ez), inner)).T, slanes, tile)
    l_fix = padded(face_sum(ex) @ np.kron(eye(ex), inner), 8 * ex, sx_rows)

    def field(rows, lanes):
        return np.broadcast_to(rows, (rows.shape[0], lanes.shape[-1])) * lanes

    def lane_of(y_part, z_part, reps=1):
        return np.tile((y_part[:, None] * z_part[None, :]).reshape(1, -1), (1, reps))

    ones = np.ones
    zsel = np.repeat(np.arange(ez), 12)
    g_tab = np.stack(
        [
            padded(
                field(np.tile(gauss, ex)[:, None], lane_of(gauss, np.tile(gauss, ez))),
                gx_rows,
                glanes,
            ),
            padded(field(ones((gx_rows, 1)), lane_of(ones(12), zsel)), gx_rows, glanes),
            padded(
                field((np.arange(gx_rows) // 12)[:, None], ones((1, glanes))),
                gx_rows,
                glanes,
            ),
        ]
    )
    zspec = np.repeat(np.arange(ez), 10)
    xspec = np.minimum(np.arange(sx_rows) // 10, ex - 1)[:, None]
    s_tab = np.stack(
        [
            padded(field(np.tile(lam, ex)[:, None], ones((1, slanes))), sx_rows, slanes, 1.0),
            padded(field(ones((sx_rows, 1)), lane_of(lam, ones(10 * ez))), sx_rows, slanes, 1.0),
            padded(
                field(ones((sx_rows, 1)), lane_of(ones(10), np.tile(lam, ez))),
                sx_rows,
                slanes,
                1.0,
            ),
            padded(field(ones((sx_rows, 1)), lane_of(ones(10), zspec)), sx_rows, slanes),
            field(xspec, ones((1, slanes))),
        ]
    )
    wi = np.tile(gll, ex + 2)[:, None]
    wz = np.tile(gll, ez)
    one_x = ones((ring_x, 1))
    wj_l = lane_of(gll, ones(nz), ey + 2)
    wk_l = lane_of(ones(8), wz, ey + 2)

    def inside(count):
        out = ones(8 * count)
        for face in range(1, count):
            out[8 * face - 1 : 8 * face + 1] = 2.0
        return np.concatenate([out[-8:], out, out[:8]])

    many = lane_of(inside(ey), ones(nz))
    znode = np.arange(nz)
    zlow = ((znode % 8 == 7) & (znode < nz - 1)).astype(np.float64)
    zhigh = ((znode % 8 == 0) & (znode > 0)).astype(np.float64)
    xs = np.zeros(ring_x)
    xh = np.zeros(ring_x)
    for edge in (8, 8 * (ex + 1)):
        xs[edge - 1] = 1.0
        xh[edge] = 1.0
    ys = np.zeros(8 * (ey + 2))
    yh = np.zeros(8 * (ey + 2))
    for edge in (8, 8 * (ey + 1)):
        ys[edge - 1] = 1.0
        yh[edge] = 1.0
    full = lane_of(ones(8), ones(nz), ey + 2)
    ring = np.stack(
        [
            field(one_x, wj_l * wk_l),
            field(wi, wk_l),
            field(wi, wj_l),
            field(wi, wj_l * wk_l),
            field(inside(ex)[:, None], many),
            field(one_x, lane_of(ones(8), np.repeat(np.arange(ez), 8), ey + 2)),
            field(one_x, wk_l),
            field(one_x, lane_of(ones(8), zlow, ey + 2)),
            field(one_x, lane_of(ones(8), zhigh, ey + 2)),
            field(xs[:, None], full),
            field(xh[:, None], full),
            field(one_x, lane_of(ys, ones(nz))),
            field(one_x, lane_of(yh, ones(nz))),
        ]
    )
    own = 8 * ex
    x_own = np.stack(
        [
            np.broadcast_to(v[:, None], (own, 128))
            for v in (
                np.tile(gll, ex),
                np.arange(own) // 8,
                face_sum(ex)[np.arange(own), np.arange(own) ^ 0] * 0.0
                + ((np.arange(own) % 8 == 7) & (np.arange(own) < own - 1)),
                ((np.arange(own) % 8 == 0) & (np.arange(own) > 0)).astype(np.float64),
            )
        ]
    )
    ynode = np.arange(8 * ey)
    y_own = np.stack(
        [
            np.broadcast_to(lane_of(v.astype(np.float64), ones(nz)), (8, 8 * ey * nz))
            for v in (
                np.tile(gll, ey),
                ynode // 8,
                (ynode % 8 == 7) & (ynode < 8 * ey - 1),
                (ynode % 8 == 0) & (ynode > 0),
            )
        ]
    )
    mats = [
        halves(m)
        for m in (
            l_in,
            r_in,
            r_back,
            l_back,
            l_div,
            l_lap,
            r_div_y,
            r_div_z,
            r_lap_y,
            r_lap_z,
            l_spec,
            r_spec,
            r_fix,
            l_fix,
        )
    ]
    tabs = [np.asarray(t, np.float32) for t in (g_tab, s_tab, ring, x_own, y_own)]
    return mats + tabs


def dot(a, b):
    return jnp.dot(a, b, preferred_element_type=F32)


def split(value):
    high = value.astype(BF16)
    return high, (value - high.astype(F32)).astype(BF16)


def times(value, table):
    high, low = split(value)
    return dot(high, table[0]) + (dot(high, table[1]) + dot(low, table[0]))


def table_times(table, value):
    high, low = split(value)
    return dot(table[0], high) + (dot(table[1], high) + dot(table[0], low))


def kernel(ex, ey, ez, n_x, n_y, *refs):
    (xs_ref, ys_ref, zs_ref, count_ref, vel_ref) = refs[:5]
    (
        l_in,
        r_in,
        r_back,
        l_back,
        l_div,
        l_lap,
        r_div_y,
        r_div_z,
        r_lap_y,
        r_lap_z,
        l_spec,
        r_spec,
        r_fix,
        l_fix,
        g_tab,
        s_tab,
        ring,
        x_own,
        y_own,
    ) = refs[5:24]
    adv_ref, press_ref = refs[24:26]
    e_vel, e_gx, e_gy, e_weak, e_fix1, e_fix2, send, recv = refs[26:]
    nx, nz = 8 * ex, 8 * ez
    tile = 8 * nz
    lanes = ey * tile
    rows = nx + 16
    wide = lanes + 2 * tile
    mx, my = lax.axis_index("gx"), lax.axis_index("gy")

    def peer(dx, dy):
        return (lax.rem(mx + dx + n_x, n_x), lax.rem(my + dy + n_y, n_y))

    sides = [(dx, dy) for dx in (-1, 1, 0) for dy in (-1, 1, 0) if (dx, dy) != (0, 0)]

    barrier = pltpu.get_barrier_semaphore()
    for dx, dy in sides:
        pl.semaphore_signal(barrier, inc=1, device_id=peer(dx, dy), device_id_type=MESH)

    def x_span(dx):
        if dx == 0:
            return (8, nx), 8
        return ((nx, 8), 0) if dx > 0 else ((8, 8), nx + 8)

    def y_span(dy):
        if dy == 0:
            return (tile, lanes), tile
        return ((lanes, tile), 0) if dy > 0 else ((tile, tile), lanes + tile)

    slot = [0]

    def send_one(make, dx, dy):
        index = slot[0]
        slot[0] += 1
        src, dst = make(dx, dy)
        copy = pltpu.make_async_remote_copy(
            src_ref=src,
            dst_ref=dst,
            send_sem=send.at[index],
            recv_sem=recv.at[index],
            device_id=peer(dx, dy),
            device_id_type=MESH,
        )
        copy.start()
        return copy

    def block(ref):
        def make(dx, dy):
            (r0, rn), rd = x_span(dx)
            (c0, cn), cd = y_span(dy)
            lead = (slice(None),) * (len(ref.shape) - 2)
            return (
                ref.at[lead + (pl.ds(r0, rn), pl.ds(c0, cn))],
                ref.at[lead + (pl.ds(rd, rn), pl.ds(cd, cn))],
            )

        return make

    def exchange(ref):
        return [send_one(block(ref), dx, dy) for dx, dy in sides]

    def only_x(dx, dy):
        (r0, rn), rd = x_span(dx)
        return e_gx.at[:, pl.ds(r0, rn), :], e_gx.at[:, pl.ds(rd, rn), :]

    def only_y(dx, dy):
        (c0, cn), cd = y_span(dy)
        return e_gy.at[:, :, pl.ds(c0, cn)], e_gy.at[:, :, pl.ds(cd, cn)]

    def pick(which, sizes, count):
        out = jnp.where(which > 0.5, sizes[1], sizes[0]) if count > 1 else sizes[0]
        for elem in range(2, count):
            out = jnp.where(which > elem - 0.5, sizes[elem], out)
        return out

    xs = [xs_ref[e] for e in range(ex)]
    ys = [ys_ref[e] for e in range(ey)]
    zs = [zs_ref[e] for e in range(ez)]
    count = count_ref[0, 0].astype(F32)

    vel = vel_ref[...]
    for c in range(3):
        e_vel[c, 8 : 8 + nx, tile : tile + lanes] = vel[c * nx : (c + 1) * nx]
    own_layer = ring[5, 8 : 8 + nx, tile : tile + lanes]
    e_vel[3, 8 : 8 + nx, tile : tile + lanes] = jnp.where(own_layer < count, 1.0, 0.0)
    hx = pick(x_own[1], xs, ex)
    part = hx * x_own[0]
    e_gx[0, 8 : 8 + nx, :] = hx
    e_gx[1, 8 : 8 + nx, :] = (
        part + x_own[2] * pltpu.roll(part, nx - 1, 0) + x_own[3] * pltpu.roll(part, 1, 0)
    )
    hy = pick(y_own[1], ys, ey)
    part = hy * y_own[0]
    e_gy[0, :, tile : tile + lanes] = hy
    e_gy[1, :, tile : tile + lanes] = (
        part + y_own[2] * pltpu.roll(part, lanes - nz, 1) + y_own[3] * pltpu.roll(part, nz, 1)
    )

    rows_g = g_tab.shape[1]
    wide_g = g_tab.shape[2]
    at_x = table_times(l_in, vel)
    by_tile = [at_x[:, f * tile : (f + 1) * tile] for f in range(ey)]
    both = times(jnp.concatenate(by_tile, axis=0), r_in.at[:, :, :wide_g])
    others = times(
        jnp.concatenate([t[: 3 * rows_g] for t in by_tile], axis=0), r_in.at[:, :, wide_g:]
    )

    pl.semaphore_wait(barrier, len(sides))
    first = exchange(e_vel)
    first += [send_one(only_x, 1, 0), send_one(only_x, -1, 0)]
    first += [send_one(only_y, 0, 1), send_one(only_y, 0, -1)]

    layer_g = g_tab[1]
    alpha = g_tab[0] * jnp.where(layer_g < count, 0.25, 0.0)
    hx_g = pick(g_tab[2], xs, ex)
    hz_g = pick(layer_g, zs, ez)
    pieces = []
    for f in range(ey):
        base = f * 6 * rows_g
        u = [both[base + c * rows_g : base + (c + 1) * rows_g] for c in range(3)]
        s0 = u[0] * (alpha * hz_g * ys[f])
        s1 = u[1] * (alpha * hz_g * hx_g)
        s2 = u[2] * (alpha * hx_g * ys[f])
        for c in range(3):
            at = f * 3 * rows_g + c * rows_g
            in_x = both[base + (3 + c) * rows_g : base + (4 + c) * rows_g]
            in_y = others[at : at + rows_g, :wide_g]
            in_z = others[at : at + rows_g, wide_g:]
            pieces.append(s0 * in_x + s1 * in_y + s2 * in_z)
    back = times(jnp.concatenate(pieces, axis=0), r_back)
    back = jnp.concatenate(
        [back[f * 3 * rows_g : (f + 1) * 3 * rows_g] for f in range(ey)], axis=1
    )
    weak = table_times(l_back, back)
    in_low = jnp.concatenate([y_own[2]] * (3 * nx // 8), axis=0)
    in_high = jnp.concatenate([y_own[3]] * (3 * nx // 8), axis=0)

    def inner_faces(value, low, high):
        return (
            value
            + low * pltpu.roll(value, lanes - nz, 1)
            + high * pltpu.roll(value, nz, 1)
        )

    weak = inner_faces(weak, in_low, in_high)
    for c in range(3):
        e_weak[c, 8 : 8 + nx, tile : tile + lanes] = weak[c * nx : (c + 1) * nx]
    second = exchange(e_weak)

    def cross(value):
        value = (
            value
            + ring[9] * pltpu.roll(value, rows - 1, 0)
            + ring[10] * pltpu.roll(value, 1, 0)
        )
        return (
            value
            + ring[11] * pltpu.roll(value, wide - nz, 1)
            + ring[12] * pltpu.roll(value, nz, 1)
        )

    def pair_z(value):
        return (
            value + ring[7] * pltpu.roll(value, wide - 1, 1) + ring[8] * pltpu.roll(value, 1, 1)
        )

    for copy in first:
        copy.wait_recv()
    mask = e_vel[3]
    hz_r = pick(ring[5], zs, ez)

    def on_rows(piece):
        return jnp.concatenate([piece] * (wide // 128), axis=1)

    def on_lanes(piece):
        return jnp.concatenate([piece] * (rows // 8), axis=0)

    hx_r = on_rows(e_gx[0])
    hy_r = on_lanes(e_gy[0])
    lumped = cross(on_rows(e_gx[1]) * on_lanes(e_gy[1]) * pair_z(mask * hz_r * ring[6]) * 0.125)
    inv_lumped = time_step / jnp.where(lumped > 0.0, lumped, 1.0)
    mult = cross(ring[4] * pair_z(mask))
    inv_mult = mask / jnp.maximum(mult, 1.0)
    quarter = (-0.25 * mask) * ring[3]
    c_x, c_y, c_z = quarter * hy_r * hz_r, quarter * hx_r * hz_r, quarter * hx_r * hy_r
    k_x = mask * (hy_r * hz_r / (2.0 * hx_r)) * ring[0]
    k_y = mask * (hx_r * hz_r / (2.0 * hy_r)) * ring[1]
    k_z = mask * (hx_r * hy_r / (2.0 * hz_r)) * ring[2]
    layer_s = s_tab[3]
    hx_s = pick(s_tab[4], xs, ex)
    hz_s = pick(layer_s, zs, ez)
    keep = jnp.where(layer_s < count, 1.0, 0.0)
    scales = []
    for f in range(ey):
        denom = ys[f] * hz_s / (2.0 * hx_s) * s_tab[0]
        denom = denom + hx_s * hz_s / (2.0 * ys[f]) * s_tab[1]
        denom = denom + hx_s * ys[f] / (2.0 * hz_s) * s_tab[2]
        scales.append(keep / denom)
    scale = jnp.concatenate(scales, axis=0)
    rows_s = s_tab.shape[1]

    def stacked(value):
        return jnp.concatenate(
            [value[:, t * tile : (t + 1) * tile] for t in range(ey + 2)], axis=0
        )

    def unstacked(value):
        return jnp.concatenate(
            [value[t * rows : (t + 1) * rows] for t in range(ey + 2)], axis=1
        )

    def schwarz(raw, target):
        spec_x = table_times(l_spec, raw)
        spec_x = jnp.concatenate(
            [spec_x[:, f * tile : (f + 3) * tile] for f in range(ey)], axis=0
        )
        spec = times(spec_x, r_spec) * scale
        fixed = times(spec, r_fix)
        fixed = jnp.concatenate(
            [fixed[f * rows_s : (f + 1) * rows_s] for f in range(ey)], axis=1
        )
        fixed = table_times(l_fix, fixed)
        fixed = inner_faces(fixed, in_low[:nx], in_high[:nx])
        target[8 : 8 + nx, tile : tile + lanes] = fixed
        return exchange(target)

    for copy in second:
        copy.wait_recv()
    adv = [(e_vel[c] - cross(e_weak[c]) * inv_lumped) * mask for c in range(3)]
    for c in range(3):
        adv_ref[c * nx : (c + 1) * nx, :] = adv[c][8 : 8 + nx, tile : tile + lanes]
    raw = (
        c_x * table_times(l_div, adv[0])
        + c_y * unstacked(times(stacked(adv[1]), r_div_y))
        + c_z * unstacked(times(stacked(adv[2]), r_div_z))
    )
    third = schwarz(raw, e_fix1)
    for copy in third:
        copy.wait_recv()
    press = cross(e_fix1[...]) * inv_mult
    by_y = stacked(press)
    raw = raw - (
        k_x * table_times(l_lap, press)
        + k_y * unstacked(times(by_y, r_lap_y))
        + k_z * unstacked(times(by_y, r_lap_z))
    )
    fourth = schwarz(raw, e_fix2)
    for copy in fourth:
        copy.wait_recv()
    press = press + cross(e_fix2[...]) * inv_mult
    press_ref[...] = press[8 : 8 + nx, tile : tile + lanes]
    for copy in first + second + third + fourth:
        copy.wait_send()


def local(n_x, n_y, velocity, x_sizes, y_sizes, z_sizes, layer_counts):
    ex, ey, ez = x_sizes.shape[0], y_sizes.shape[0], z_sizes.shape[0]
    nx, ny, nz = 8 * ex, 8 * ey, 8 * ez
    tile = 8 * nz
    lanes = ny * nz
    rows, wide = nx + 16, lanes + 2 * tile
    vel = velocity.transpose(2, 0, 1, 3).reshape(3 * nx, lanes)
    consts = [jnp.asarray(c) for c in constants(ex, ey, ez)]
    smem = pl.BlockSpec(memory_space=pltpu.SMEM)
    vmem = pl.BlockSpec(memory_space=pltpu.VMEM)
    copies = 4 * 8 + 4
    adv, press = pl.pallas_call(
        functools.partial(kernel, ex, ey, ez, n_x, n_y),
        out_shape=(
            jax.ShapeDtypeStruct((3 * nx, lanes), F32),
            jax.ShapeDtypeStruct((nx, lanes), F32),
        ),
        in_specs=[smem] * 4 + [vmem] * (1 + len(consts)),
        out_specs=(vmem, vmem),
        scratch_shapes=[
            pltpu.VMEM((4, rows, wide), F32),
            pltpu.VMEM((2, rows, 128), F32),
            pltpu.VMEM((2, 8, wide), F32),
            pltpu.VMEM((3, rows, wide), F32),
            pltpu.VMEM((rows, wide), F32),
            pltpu.VMEM((rows, wide), F32),
            pltpu.SemaphoreType.DMA((copies,)),
            pltpu.SemaphoreType.DMA((copies,)),
        ],
        compiler_params=pltpu.CompilerParams(collective_id=0, has_side_effects=True),
        name="sem_step",
    )(x_sizes, y_sizes, z_sizes, layer_counts, vel, *consts)
    advected = adv.reshape(3, nx, ny, nz).transpose(1, 2, 0, 3)
    return advected, press.reshape(nx, ny, nz)


def solution(mesh):
    in_specs = (P("gx", "gy", None, None), P("gx"), P("gy"), P(), P("gx", "gy"))
    out_specs = (P("gx", "gy", None, None), P("gx", "gy", None))
    body = functools.partial(local, mesh.shape["gx"], mesh.shape["gy"])
    return jax.shard_map(body, mesh=mesh, in_specs=in_specs, out_specs=out_specs, check_vma=False)
```

```python
import functools
import math

import jax
import jax.numpy as jnp
import numpy as np
from jax import lax
from jax.experimental import pallas as pl
from jax.experimental.pallas import tpu as pltpu
from jax.sharding import PartitionSpec as P

SWEEPS = 2
time_step = 0.005
MESH = pl.DeviceIdType.MESH
F32 = jnp.float32
BF16 = jnp.bfloat16


def legendre_value(order, point):
    previous = 1.0
    current = point
    for degree in range(2, order + 1):
        previous, current = (
            current,
            ((2 * degree - 1) * point * current - (degree - 1) * previous) / degree,
        )
    return current


def legendre_pair(order, point):
    previous = 1.0
    current = point
    for degree in range(2, order + 1):
        previous, current = (
            current,
            ((2 * degree - 1) * point * current - (degree - 1) * previous) / degree,
        )
    slope = order * (point * current - previous) / (point * point - 1.0)
    return (current, slope)


def tables():
    inner_points = []
    for index in range(1, 7):
        point = -math.cos(math.pi * index / 7.0)
        for newton in range(60):
            value, slope = legendre_pair(7, point)
            curvature = (2.0 * point * slope - 56.0 * value) / (1.0 - point * point)
            point = point - slope / curvature
        inner_points.append(point)
    gll_points = [-1.0] + inner_points + [1.0]
    gll_weights = [2.0 / (56.0 * legendre_value(7, point) ** 2) for point in gll_points]
    barycentric = []
    for first in range(8):
        product = 1.0
        for second in range(8):
            if second != first:
                product = product * (gll_points[first] - gll_points[second])
        barycentric.append(1.0 / product)
    derivative = [[0.0] * 8 for first in range(8)]
    for first in range(8):
        total = 0.0
        for second in range(8):
            if second != first:
                entry = (
                    barycentric[second]
                    / barycentric[first]
                    / (gll_points[first] - gll_points[second])
                )
                derivative[first][second] = entry
                total = total + entry
        derivative[first][first] = -total
    gauss_points = []
    gauss_weights = []
    for index in range(1, 13):
        point = -math.cos(math.pi * (index - 0.25) / 12.5)
        for newton in range(60):
            value, slope = legendre_pair(12, point)
            point = point - value / slope
        value, slope = legendre_pair(12, point)
        gauss_points.append(point)
        gauss_weights.append(2.0 / ((1.0 - point * point) * slope * slope))
    interpolate = []
    for gauss in gauss_points:
        fraction = [barycentric[node] / (gauss - gll_points[node]) for node in range(8)]
        total = sum(fraction)
        interpolate.append([entry / total for entry in fraction])
    stiffness = [
        [
            sum(
                (
                    derivative[inner][first] * gll_weights[inner] * derivative[inner][second]
                    for inner in range(8)
                )
            )
            for second in range(8)
        ]
        for first in range(8)
    ]
    glob_stiff = [[0.0] * 22 for first in range(22)]
    glob_mass = [0.0] * 22
    for offset in (0, 7, 14):
        for first in range(8):
            glob_mass[offset + first] = glob_mass[offset + first] + gll_weights[first]
            for second in range(8):
                glob_stiff[offset + first][offset + second] = (
                    glob_stiff[offset + first][offset + second] + stiffness[first][second]
                )
    inv_root = [1.0 / math.sqrt(glob_mass[6 + first]) for first in range(10)]
    matrix = [
        [
            inv_root[first] * glob_stiff[6 + first][6 + second] * inv_root[second]
            for second in range(10)
        ]
        for first in range(10)
    ]
    rotation = [[1.0 if first == second else 0.0 for second in range(10)] for first in range(10)]
    for sweep in range(20):
        for first in range(10):
            for second in range(first + 1, 10):
                angle = 0.5 * math.atan2(
                    2.0 * matrix[first][second], matrix[second][second] - matrix[first][first]
                )
                cosine = math.cos(angle)
                sine = math.sin(angle)
                for other in range(10):
                    left_val = matrix[other][first]
                    right_val = matrix[other][second]
                    matrix[other][first] = cosine * left_val - sine * right_val
                    matrix[other][second] = sine * left_val + cosine * right_val
                    left_val = rotation[other][first]
                    right_val = rotation[other][second]
                    rotation[other][first] = cosine * left_val - sine * right_val
                    rotation[other][second] = sine * left_val + cosine * right_val
                for other in range(10):
                    upper_val = matrix[first][other]
                    lower_val = matrix[second][other]
                    matrix[first][other] = cosine * upper_val - sine * lower_val
                    matrix[second][other] = sine * upper_val + cosine * lower_val
    eigen_values = [matrix[first][first] for first in range(10)]
    vectors = [
        [inv_root[first] * rotation[first][second] for second in range(10)] for first in range(10)
    ]
    return tuple(
        np.asarray(table, dtype=np.float64)
        for table in (
            derivative,
            gll_weights,
            interpolate,
            gauss_weights,
            stiffness,
            vectors,
            eigen_values,
        )
    )


def halves(matrix):
    matrix = np.asarray(matrix, np.float32)
    high = matrix.astype(BF16)
    low = (matrix - high.astype(np.float32)).astype(BF16)
    return np.stack([high, low])


def padded(matrix, rows, cols, fill=0.0):
    out = np.full((rows, cols), fill, np.float64)
    out[: matrix.shape[0], : matrix.shape[1]] = matrix
    return out


def face_sum(count):
    out = np.eye(8 * count)
    for face in range(1, count):
        out[8 * face - 1, 8 * face] = 1.0
        out[8 * face, 8 * face - 1] = 1.0
    return out


def up8(value, step):
    return -(-value // step) * step


def constants(ex, ey, ez):
    deriv, gll, interp, gauss, stiff, vecs, lam = tables()
    eye = np.eye
    gx_rows = up8(12 * ex, 8)
    nz = 8 * ez
    tile = 8 * nz
    glanes = up8(144 * ez, 128)
    int_d = interp @ deriv
    sum_z = face_sum(ez)
    jx = padded(np.kron(eye(ex), interp), gx_rows, 8 * ex)
    dx = padded(np.kron(eye(ex), int_d), gx_rows, 8 * ex)
    l_in = np.concatenate([np.kron(eye(3), jx), np.kron(eye(3), dx)])
    jz = np.kron(eye(ez), interp)
    dz = np.kron(eye(ez), int_d)
    r_in = np.concatenate(
        [
            padded(np.kron(a, b).T, tile, glanes)
            for a, b in ((interp, jz), (int_d, jz), (interp, dz))
        ],
        axis=1,
    )
    r_back = padded(np.kron(interp, jz @ sum_z.T), glanes, tile)
    l_back = np.kron(eye(3), face_sum(ex) @ jx.T)
    ring_x = 8 * (ex + 2)
    l_div = np.kron(eye(ex + 2), deriv)
    l_lap = np.kron(eye(ex + 2), stiff)
    r_div_y = np.kron(deriv.T, eye(nz))
    r_div_z = np.kron(eye(8), np.kron(eye(ez), deriv.T))
    r_lap_y = np.kron(stiff.T, eye(nz))
    r_lap_z = np.kron(eye(8), np.kron(eye(ez), stiff.T))
    sx_rows = up8(10 * ex, 8)

    def extend(count):
        out = np.zeros((10 * count, 8 * (count + 2)))
        for elem in range(count):
            base = 8 * (elem + 1)
            out[10 * elem, base - 2] = 1.0
            for node in range(8):
                out[10 * elem + 1 + node, base + node] = 1.0
            out[10 * elem + 9, base + 9] = 1.0
        return out

    l_spec = padded(
        np.kron(eye(ex), vecs.T) @ extend(ex) @ face_sum(ex + 2), sx_rows, ring_x
    )
    ext_y = vecs.T @ extend(1) @ face_sum(3)
    ext_z = np.kron(eye(ez), vecs.T) @ extend(ez)[:, 8:-8] @ sum_z
    slanes = up8(100 * ez, 128)
    r_spec = padded(np.kron(ext_y, ext_z).T, 3 * tile, slanes)
    inner = vecs[1:9]
    r_fix = padded(np.kron(inner, sum_z @ np.kron(eye(ez), inner)).T, slanes, tile)
    l_fix = padded(face_sum(ex) @ np.kron(eye(ex), inner), 8 * ex, sx_rows)

    def field(rows, lanes):
        return np.broadcast_to(rows, (rows.shape[0], lanes.shape[-1])) * lanes

    def lane_of(y_part, z_part, reps=1):
        return np.tile((y_part[:, None] * z_part[None, :]).reshape(1, -1), (1, reps))

    ones = np.ones
    zsel = np.repeat(np.arange(ez), 12)
    g_tab = np.stack(
        [
            padded(
                field(np.tile(gauss, ex)[:, None], lane_of(gauss, np.tile(gauss, ez))),
                gx_rows,
                glanes,
            ),
            padded(field(ones((gx_rows, 1)), lane_of(ones(12), zsel)), gx_rows, glanes),
            padded(
                field((np.arange(gx_rows) // 12)[:, None], ones((1, glanes))),
                gx_rows,
                glanes,
            ),
        ]
    )
    zspec = np.repeat(np.arange(ez), 10)
    xspec = np.minimum(np.arange(sx_rows) // 10, ex - 1)[:, None]
    s_tab = np.stack(
        [
            padded(field(np.tile(lam, ex)[:, None], ones((1, slanes))), sx_rows, slanes, 1.0),
            padded(field(ones((sx_rows, 1)), lane_of(lam, ones(10 * ez))), sx_rows, slanes, 1.0),
            padded(
                field(ones((sx_rows, 1)), lane_of(ones(10), np.tile(lam, ez))),
                sx_rows,
                slanes,
                1.0,
            ),
            padded(field(ones((sx_rows, 1)), lane_of(ones(10), zspec)), sx_rows, slanes),
            field(xspec, ones((1, slanes))),
        ]
    )
    wi = np.tile(gll, ex + 2)[:, None]
    wz = np.tile(gll, ez)
    one_x = ones((ring_x, 1))
    wj_l = lane_of(gll, ones(nz), ey + 2)
    wk_l = lane_of(ones(8), wz, ey + 2)

    def inside(count):
        out = ones(8 * count)
        for face in range(1, count):
            out[8 * face - 1 : 8 * face + 1] = 2.0
        return np.concatenate([out[-8:], out, out[:8]])

    many = lane_of(inside(ey), ones(nz))
    znode = np.arange(nz)
    zlow = ((znode % 8 == 7) & (znode < nz - 1)).astype(np.float64)
    zhigh = ((znode % 8 == 0) & (znode > 0)).astype(np.float64)
    xs = np.zeros(ring_x)
    xh = np.zeros(ring_x)
    for edge in (8, 8 * (ex + 1)):
        xs[edge - 1] = 1.0
        xh[edge] = 1.0
    ys = np.zeros(8 * (ey + 2))
    yh = np.zeros(8 * (ey + 2))
    for edge in (8, 8 * (ey + 1)):
        ys[edge - 1] = 1.0
        yh[edge] = 1.0
    full = lane_of(ones(8), ones(nz), ey + 2)
    ring = np.stack(
        [
            field(one_x, wj_l * wk_l),
            field(wi, wk_l),
            field(wi, wj_l),
            field(wi, wj_l * wk_l),
            field(inside(ex)[:, None], many),
            field(one_x, lane_of(ones(8), np.repeat(np.arange(ez), 8), ey + 2)),
            field(one_x, wk_l),
            field(one_x, lane_of(ones(8), zlow, ey + 2)),
            field(one_x, lane_of(ones(8), zhigh, ey + 2)),
            field(xs[:, None], full),
            field(xh[:, None], full),
            field(one_x, lane_of(ys, ones(nz))),
            field(one_x, lane_of(yh, ones(nz))),
        ]
    )
    own = 8 * ex
    x_own = np.stack(
        [
            np.broadcast_to(v[:, None], (own, 128))
            for v in (
                np.tile(gll, ex),
                np.arange(own) // 8,
                face_sum(ex)[np.arange(own), np.arange(own) ^ 0] * 0.0
                + ((np.arange(own) % 8 == 7) & (np.arange(own) < own - 1)),
                ((np.arange(own) % 8 == 0) & (np.arange(own) > 0)).astype(np.float64),
            )
        ]
    )
    ynode = np.arange(8 * ey)
    y_own = np.stack(
        [
            np.broadcast_to(lane_of(v.astype(np.float64), ones(nz)), (8, 8 * ey * nz))
            for v in (
                np.tile(gll, ey),
                ynode // 8,
                (ynode % 8 == 7) & (ynode < 8 * ey - 1),
                (ynode % 8 == 0) & (ynode > 0),
            )
        ]
    )
    mats = [
        halves(m)
        for m in (
            l_in,
            r_in,
            r_back,
            l_back,
            l_div,
            l_lap,
            r_div_y,
            r_div_z,
            r_lap_y,
            r_lap_z,
            l_spec,
            r_spec,
            r_fix,
            l_fix,
        )
    ]
    tabs = [np.asarray(t, np.float32) for t in (g_tab, s_tab, ring, x_own, y_own)]
    return mats + tabs


def dot(a, b):
    return jnp.dot(a, b, preferred_element_type=F32)


def split(value):
    high = value.astype(BF16)
    return high, (value - high.astype(F32)).astype(BF16)


def times(value, table):
    high, low = split(value)
    return dot(high, table[0]) + (dot(high, table[1]) + dot(low, table[0]))


def table_times(table, value):
    high, low = split(value)
    return dot(table[0], high) + (dot(table[1], high) + dot(table[0], low))


def kernel(ex, ey, ez, n_x, n_y, *refs):
    n_tab = 24
    outer, outs = refs[:n_tab], refs[n_tab : n_tab + 2]
    held = refs[n_tab + 2 : 2 * n_tab + 2]
    (xs_ref, ys_ref, zs_ref, count_ref, vel_ref) = held[:5]
    (
        l_in,
        r_in,
        r_back,
        l_back,
        l_div,
        l_lap,
        r_div_y,
        r_div_z,
        r_lap_y,
        r_lap_z,
        l_spec,
        r_spec,
        r_fix,
        l_fix,
        g_tab,
        s_tab,
        ring,
        x_own,
        y_own,
    ) = held[5:]
    adv_ref, press_ref = outs
    e_vel, e_gx, e_gy, e_weak, e_fix1, e_fix2, send, recv, load = refs[2 * n_tab + 2 :]
    nx, nz = 8 * ex, 8 * ez
    tile = 8 * nz
    lanes = ey * tile
    rows = nx + 16
    wide = lanes + 2 * tile
    mx, my = lax.axis_index("gx"), lax.axis_index("gy")

    def peer(dx, dy):
        return (lax.rem(mx + dx + n_x, n_x), lax.rem(my + dy + n_y, n_y))

    sides = [(dx, dy) for dx in (-1, 1, 0) for dy in (-1, 1, 0) if (dx, dy) != (0, 0)]

    barrier = pltpu.get_barrier_semaphore()
    for dx, dy in sides:
        pl.semaphore_signal(barrier, inc=1, device_id=peer(dx, dy), device_id_type=MESH)
    loads = [
        pltpu.make_async_copy(outer[i], held[i], load.at[i])
        for i in range(n_tab)
    ]
    for copy in loads:
        copy.start()

    def ready(*which):
        for i in which:
            loads[i].wait()


    def x_span(dx):
        if dx == 0:
            return (8, nx), 8
        return ((nx, 8), 0) if dx > 0 else ((8, 8), nx + 8)

    def y_span(dy):
        if dy == 0:
            return (tile, lanes), tile
        return ((lanes, tile), 0) if dy > 0 else ((tile, tile), lanes + tile)

    slot = [0]

    def send_one(make, dx, dy):
        index = slot[0]
        slot[0] += 1
        src, dst = make(dx, dy)
        copy = pltpu.make_async_remote_copy(
            src_ref=src,
            dst_ref=dst,
            send_sem=send.at[index],
            recv_sem=recv.at[index],
            device_id=peer(dx, dy),
            device_id_type=MESH,
        )
        copy.start()
        return copy

    def block(ref):
        def make(dx, dy):
            (r0, rn), rd = x_span(dx)
            (c0, cn), cd = y_span(dy)
            lead = (slice(None),) * (len(ref.shape) - 2)
            return (
                ref.at[lead + (pl.ds(r0, rn), pl.ds(c0, cn))],
                ref.at[lead + (pl.ds(rd, rn), pl.ds(cd, cn))],
            )

        return make

    def exchange(ref):
        return [send_one(block(ref), dx, dy) for dx, dy in sides]

    def only_x(dx, dy):
        (r0, rn), rd = x_span(dx)
        return e_gx.at[:, pl.ds(r0, rn), :], e_gx.at[:, pl.ds(rd, rn), :]

    def only_y(dx, dy):
        (c0, cn), cd = y_span(dy)
        return e_gy.at[:, :, pl.ds(c0, cn)], e_gy.at[:, :, pl.ds(cd, cn)]

    def pick(which, sizes, count):
        out = jnp.where(which > 0.5, sizes[1], sizes[0]) if count > 1 else sizes[0]
        for elem in range(2, count):
            out = jnp.where(which > elem - 0.5, sizes[elem], out)
        return out

    ready(*range(5), 21, 22, 23)
    xs = [xs_ref[e] for e in range(ex)]
    ys = [ys_ref[e] for e in range(ey)]
    zs = [zs_ref[e] for e in range(ez)]
    count = count_ref[0, 0].astype(F32)

    ny = 8 * ey
    vel = jnp.concatenate(
        [
            jnp.concatenate(
                [vel_ref[pl.ds(c * ny + y, nx, stride=3 * ny), :] for y in range(ny)], axis=1
            )
            for c in range(3)
        ],
        axis=0,
    )
    for c in range(3):
        e_vel[c, 8 : 8 + nx, tile : tile + lanes] = vel[c * nx : (c + 1) * nx]
    own_layer = ring[5, 8 : 8 + nx, tile : tile + lanes]
    e_vel[3, 8 : 8 + nx, tile : tile + lanes] = jnp.where(own_layer < count, 1.0, 0.0)
    hx = pick(x_own[1], xs, ex)
    part = hx * x_own[0]
    e_gx[0, 8 : 8 + nx, :] = hx
    e_gx[1, 8 : 8 + nx, :] = (
        part + x_own[2] * pltpu.roll(part, nx - 1, 0) + x_own[3] * pltpu.roll(part, 1, 0)
    )
    hy = pick(y_own[1], ys, ey)
    part = hy * y_own[0]
    e_gy[0, :, tile : tile + lanes] = hy
    e_gy[1, :, tile : tile + lanes] = (
        part + y_own[2] * pltpu.roll(part, lanes - nz, 1) + y_own[3] * pltpu.roll(part, nz, 1)
    )

    rows_g = g_tab.shape[1]
    wide_g = g_tab.shape[2]
    ready(5, 6, 19)
    at_x = table_times(l_in, vel)
    by_tile = [at_x[:, f * tile : (f + 1) * tile] for f in range(ey)]
    both = times(jnp.concatenate(by_tile, axis=0), r_in.at[:, :, :wide_g])
    others = times(
        jnp.concatenate([t[: 3 * rows_g] for t in by_tile], axis=0), r_in.at[:, :, wide_g:]
    )

    pl.semaphore_wait(barrier, len(sides))
    first = exchange(e_vel)
    first += [send_one(only_x, 1, 0), send_one(only_x, -1, 0)]
    first += [send_one(only_y, 0, 1), send_one(only_y, 0, -1)]

    layer_g = g_tab[1]
    alpha = g_tab[0] * jnp.where(layer_g < count, 0.25, 0.0)
    hx_g = pick(g_tab[2], xs, ex)
    hz_g = pick(layer_g, zs, ez)
    pieces = []
    for f in range(ey):
        base = f * 6 * rows_g
        u = [both[base + c * rows_g : base + (c + 1) * rows_g] for c in range(3)]
        s0 = u[0] * (alpha * hz_g * ys[f])
        s1 = u[1] * (alpha * hz_g * hx_g)
        s2 = u[2] * (alpha * hx_g * ys[f])
        for c in range(3):
            at = f * 3 * rows_g + c * rows_g
            in_x = both[base + (3 + c) * rows_g : base + (4 + c) * rows_g]
            in_y = others[at : at + rows_g, :wide_g]
            in_z = others[at : at + rows_g, wide_g:]
            pieces.append(s0 * in_x + s1 * in_y + s2 * in_z)
    ready(7, 8)
    back = times(jnp.concatenate(pieces, axis=0), r_back)
    back = jnp.concatenate(
        [back[f * 3 * rows_g : (f + 1) * 3 * rows_g] for f in range(ey)], axis=1
    )
    weak = table_times(l_back, back)
    in_low = jnp.concatenate([y_own[2]] * (3 * nx // 8), axis=0)
    in_high = jnp.concatenate([y_own[3]] * (3 * nx // 8), axis=0)

    def inner_faces(value, low, high):
        return (
            value
            + low * pltpu.roll(value, lanes - nz, 1)
            + high * pltpu.roll(value, nz, 1)
        )

    weak = inner_faces(weak, in_low, in_high)
    for c in range(3):
        e_weak[c, 8 : 8 + nx, tile : tile + lanes] = weak[c * nx : (c + 1) * nx]
    second = exchange(e_weak)

    def cross(value):
        value = (
            value
            + ring[9] * pltpu.roll(value, rows - 1, 0)
            + ring[10] * pltpu.roll(value, 1, 0)
        )
        return (
            value
            + ring[11] * pltpu.roll(value, wide - nz, 1)
            + ring[12] * pltpu.roll(value, nz, 1)
        )

    def pair_z(value):
        return (
            value + ring[7] * pltpu.roll(value, wide - 1, 1) + ring[8] * pltpu.roll(value, 1, 1)
        )

    ready(*range(9, 19), 20)
    for copy in first:
        copy.wait_recv()
    mask = e_vel[3]
    hz_r = pick(ring[5], zs, ez)

    def on_rows(piece):
        return jnp.concatenate([piece] * (wide // 128), axis=1)

    def on_lanes(piece):
        return jnp.concatenate([piece] * (rows // 8), axis=0)

    hx_r = on_rows(e_gx[0])
    hy_r = on_lanes(e_gy[0])
    lumped = cross(on_rows(e_gx[1]) * on_lanes(e_gy[1]) * pair_z(mask * hz_r * ring[6]) * 0.125)
    inv_lumped = time_step / jnp.where(lumped > 0.0, lumped, 1.0)
    mult = cross(ring[4] * pair_z(mask))
    inv_mult = mask / jnp.maximum(mult, 1.0)
    quarter = (-0.25 * mask) * ring[3]
    c_x, c_y, c_z = quarter * hy_r * hz_r, quarter * hx_r * hz_r, quarter * hx_r * hy_r
    k_x = mask * (hy_r * hz_r / (2.0 * hx_r)) * ring[0]
    k_y = mask * (hx_r * hz_r / (2.0 * hy_r)) * ring[1]
    k_z = mask * (hx_r * hy_r / (2.0 * hz_r)) * ring[2]
    layer_s = s_tab[3]
    hx_s = pick(s_tab[4], xs, ex)
    hz_s = pick(layer_s, zs, ez)
    keep = jnp.where(layer_s < count, 1.0, 0.0)
    scales = []
    for f in range(ey):
        denom = ys[f] * hz_s / (2.0 * hx_s) * s_tab[0]
        denom = denom + hx_s * hz_s / (2.0 * ys[f]) * s_tab[1]
        denom = denom + hx_s * ys[f] / (2.0 * hz_s) * s_tab[2]
        scales.append(keep / denom)
    scale = jnp.concatenate(scales, axis=0)
    rows_s = s_tab.shape[1]

    def stacked(value):
        return jnp.concatenate(
            [value[:, t * tile : (t + 1) * tile] for t in range(ey + 2)], axis=0
        )

    def unstacked(value):
        return jnp.concatenate(
            [value[t * rows : (t + 1) * rows] for t in range(ey + 2)], axis=1
        )

    def schwarz(raw, target):
        spec_x = table_times(l_spec, raw)
        spec_x = jnp.concatenate(
            [spec_x[:, f * tile : (f + 3) * tile] for f in range(ey)], axis=0
        )
        spec = times(spec_x, r_spec) * scale
        fixed = times(spec, r_fix)
        fixed = jnp.concatenate(
            [fixed[f * rows_s : (f + 1) * rows_s] for f in range(ey)], axis=1
        )
        fixed = table_times(l_fix, fixed)
        fixed = inner_faces(fixed, in_low[:nx], in_high[:nx])
        target[8 : 8 + nx, tile : tile + lanes] = fixed
        return exchange(target)

    for copy in second:
        copy.wait_recv()
    adv = [(e_vel[c] - cross(e_weak[c]) * inv_lumped) * mask for c in range(3)]
    raw = (
        c_x * table_times(l_div, adv[0])
        + c_y * unstacked(times(stacked(adv[1]), r_div_y))
        + c_z * unstacked(times(stacked(adv[2]), r_div_z))
    )
    third = schwarz(raw, e_fix1)
    for c in range(3):
        own = adv[c][8 : 8 + nx, tile : tile + lanes]
        for y in range(ny):
            adv_ref[pl.ds(c * ny + y, nx, stride=3 * ny), :] = own[:, y * nz : (y + 1) * nz]
    for copy in third:
        copy.wait_recv()
    press = cross(e_fix1[...]) * inv_mult
    by_y = stacked(press)
    raw = raw - (
        k_x * table_times(l_lap, press)
        + k_y * unstacked(times(by_y, r_lap_y))
        + k_z * unstacked(times(by_y, r_lap_z))
    )
    fourth = schwarz(raw, e_fix2)
    for copy in fourth:
        copy.wait_recv()
    press = press + cross(e_fix2[...]) * inv_mult
    own = press[8 : 8 + nx, tile : tile + lanes]
    for y in range(ny):
        press_ref[pl.ds(y, nx, stride=ny), :] = own[:, y * nz : (y + 1) * nz]
    for copy in first + second + third + fourth:
        copy.wait_send()


def local(n_x, n_y, velocity, x_sizes, y_sizes, z_sizes, layer_counts):
    ex, ey, ez = x_sizes.shape[0], y_sizes.shape[0], z_sizes.shape[0]
    nx, ny, nz = 8 * ex, 8 * ey, 8 * ez
    tile = 8 * nz
    lanes = ny * nz
    rows, wide = nx + 16, lanes + 2 * tile
    vel = velocity.transpose(0, 2, 1, 3).reshape(3 * nx * ny, nz)
    consts = [jnp.asarray(c) for c in constants(ex, ey, ez)]
    vmem = pl.BlockSpec(memory_space=pltpu.VMEM)
    copies = 4 * 8 + 4
    scalars = (x_sizes, y_sizes, z_sizes, layer_counts)
    tables_in = (vel, *consts)
    adv, press = pl.pallas_call(
        functools.partial(kernel, ex, ey, ez, n_x, n_y),
        out_shape=(
            jax.ShapeDtypeStruct((3 * nx * ny, nz), F32),
            jax.ShapeDtypeStruct((nx * ny, nz), F32),
        ),
        in_specs=[pl.BlockSpec(memory_space=pl.ANY)] * (4 + len(tables_in)),
        out_specs=(vmem, vmem),
        scratch_shapes=[pltpu.SMEM(a.shape, a.dtype) for a in scalars]
        + [pltpu.VMEM(a.shape, a.dtype) for a in tables_in]
        + [
            pltpu.VMEM((4, rows, wide), F32),
            pltpu.VMEM((2, rows, 128), F32),
            pltpu.VMEM((2, 8, wide), F32),
            pltpu.VMEM((3, rows, wide), F32),
            pltpu.VMEM((rows, wide), F32),
            pltpu.VMEM((rows, wide), F32),
            pltpu.SemaphoreType.DMA((copies,)),
            pltpu.SemaphoreType.DMA((copies,)),
            pltpu.SemaphoreType.DMA((4 + len(tables_in),)),
        ],
        compiler_params=pltpu.CompilerParams(collective_id=0, has_side_effects=True),
        name="sem_step",
    )(*scalars, *tables_in)
    advected = adv.reshape(nx, 3, ny, nz).transpose(0, 2, 1, 3)
    return advected, press.reshape(nx, ny, nz)


def solution(mesh):
    in_specs = (P("gx", "gy", None, None), P("gx"), P("gy"), P(), P("gx", "gy"))
    out_specs = (P("gx", "gy", None, None), P("gx", "gy", None))
    body = functools.partial(local, mesh.shape["gx"], mesh.shape["gy"])
    return jax.shard_map(body, mesh=mesh, in_specs=in_specs, out_specs=out_specs, check_vma=False)
```

```python
import functools
import math

import jax
import jax.numpy as jnp
import numpy as np
from jax import lax
from jax.experimental import pallas as pl
from jax.experimental.pallas import tpu as pltpu
from jax.sharding import PartitionSpec as P

SWEEPS = 2
time_step = 0.005
MESH = pl.DeviceIdType.MESH
F32 = jnp.float32
BF16 = jnp.bfloat16


def legendre_value(order, point):
    previous = 1.0
    current = point
    for degree in range(2, order + 1):
        previous, current = (
            current,
            ((2 * degree - 1) * point * current - (degree - 1) * previous) / degree,
        )
    return current


def legendre_pair(order, point):
    previous = 1.0
    current = point
    for degree in range(2, order + 1):
        previous, current = (
            current,
            ((2 * degree - 1) * point * current - (degree - 1) * previous) / degree,
        )
    slope = order * (point * current - previous) / (point * point - 1.0)
    return (current, slope)


def tables():
    inner_points = []
    for index in range(1, 7):
        point = -math.cos(math.pi * index / 7.0)
        for newton in range(60):
            value, slope = legendre_pair(7, point)
            curvature = (2.0 * point * slope - 56.0 * value) / (1.0 - point * point)
            point = point - slope / curvature
        inner_points.append(point)
    gll_points = [-1.0] + inner_points + [1.0]
    gll_weights = [2.0 / (56.0 * legendre_value(7, point) ** 2) for point in gll_points]
    barycentric = []
    for first in range(8):
        product = 1.0
        for second in range(8):
            if second != first:
                product = product * (gll_points[first] - gll_points[second])
        barycentric.append(1.0 / product)
    derivative = [[0.0] * 8 for first in range(8)]
    for first in range(8):
        total = 0.0
        for second in range(8):
            if second != first:
                entry = (
                    barycentric[second]
                    / barycentric[first]
                    / (gll_points[first] - gll_points[second])
                )
                derivative[first][second] = entry
                total = total + entry
        derivative[first][first] = -total
    gauss_points = []
    gauss_weights = []
    for index in range(1, 13):
        point = -math.cos(math.pi * (index - 0.25) / 12.5)
        for newton in range(60):
            value, slope = legendre_pair(12, point)
            point = point - value / slope
        value, slope = legendre_pair(12, point)
        gauss_points.append(point)
        gauss_weights.append(2.0 / ((1.0 - point * point) * slope * slope))
    interpolate = []
    for gauss in gauss_points:
        fraction = [barycentric[node] / (gauss - gll_points[node]) for node in range(8)]
        total = sum(fraction)
        interpolate.append([entry / total for entry in fraction])
    stiffness = [
        [
            sum(
                (
                    derivative[inner][first] * gll_weights[inner] * derivative[inner][second]
                    for inner in range(8)
                )
            )
            for second in range(8)
        ]
        for first in range(8)
    ]
    glob_stiff = [[0.0] * 22 for first in range(22)]
    glob_mass = [0.0] * 22
    for offset in (0, 7, 14):
        for first in range(8):
            glob_mass[offset + first] = glob_mass[offset + first] + gll_weights[first]
            for second in range(8):
                glob_stiff[offset + first][offset + second] = (
                    glob_stiff[offset + first][offset + second] + stiffness[first][second]
                )
    inv_root = [1.0 / math.sqrt(glob_mass[6 + first]) for first in range(10)]
    matrix = [
        [
            inv_root[first] * glob_stiff[6 + first][6 + second] * inv_root[second]
            for second in range(10)
        ]
        for first in range(10)
    ]
    rotation = [[1.0 if first == second else 0.0 for second in range(10)] for first in range(10)]
    for sweep in range(20):
        for first in range(10):
            for second in range(first + 1, 10):
                angle = 0.5 * math.atan2(
                    2.0 * matrix[first][second], matrix[second][second] - matrix[first][first]
                )
                cosine = math.cos(angle)
                sine = math.sin(angle)
                for other in range(10):
                    left_val = matrix[other][first]
                    right_val = matrix[other][second]
                    matrix[other][first] = cosine * left_val - sine * right_val
                    matrix[other][second] = sine * left_val + cosine * right_val
                    left_val = rotation[other][first]
                    right_val = rotation[other][second]
                    rotation[other][first] = cosine * left_val - sine * right_val
                    rotation[other][second] = sine * left_val + cosine * right_val
                for other in range(10):
                    upper_val = matrix[first][other]
                    lower_val = matrix[second][other]
                    matrix[first][other] = cosine * upper_val - sine * lower_val
                    matrix[second][other] = sine * upper_val + cosine * lower_val
    eigen_values = [matrix[first][first] for first in range(10)]
    vectors = [
        [inv_root[first] * rotation[first][second] for second in range(10)] for first in range(10)
    ]
    return tuple(
        np.asarray(table, dtype=np.float64)
        for table in (
            derivative,
            gll_weights,
            interpolate,
            gauss_weights,
            stiffness,
            vectors,
            eigen_values,
        )
    )


def halves(matrix):
    matrix = np.asarray(matrix, np.float32)
    high = matrix.astype(BF16)
    low = (matrix - high.astype(np.float32)).astype(BF16)
    return np.stack([high, low])


def padded(matrix, rows, cols, fill=0.0):
    out = np.full((rows, cols), fill, np.float64)
    out[: matrix.shape[0], : matrix.shape[1]] = matrix
    return out


def face_sum(count):
    out = np.eye(8 * count)
    for face in range(1, count):
        out[8 * face - 1, 8 * face] = 1.0
        out[8 * face, 8 * face - 1] = 1.0
    return out


def up8(value, step):
    return -(-value // step) * step


def constants(ex, ey, ez):
    deriv, gll, interp, gauss, stiff, vecs, lam = tables()
    eye = np.eye
    gx_rows = up8(12 * ex, 8)
    nz = 8 * ez
    tile = 8 * nz
    glanes = up8(144 * ez, 128)
    int_d = interp @ deriv
    sum_z = face_sum(ez)
    jx = padded(np.kron(eye(ex), interp), gx_rows, 8 * ex)
    dx = padded(np.kron(eye(ex), int_d), gx_rows, 8 * ex)
    l_in = np.concatenate([np.kron(eye(3), jx), np.kron(eye(3), dx)])
    jz = np.kron(eye(ez), interp)
    dz = np.kron(eye(ez), int_d)
    r_in = np.concatenate(
        [
            padded(np.kron(a, b).T, tile, glanes)
            for a, b in ((interp, jz), (int_d, jz), (interp, dz))
        ],
        axis=1,
    )
    r_back = padded(np.kron(interp, jz @ sum_z.T), glanes, tile)
    l_back = np.kron(eye(3), face_sum(ex) @ jx.T)
    ring_x = 8 * (ex + 2)
    l_div = np.kron(eye(ex + 2), deriv)
    l_lap = np.kron(eye(ex + 2), stiff)
    r_div_y = np.kron(deriv.T, eye(nz))
    r_div_z = np.kron(eye(8), np.kron(eye(ez), deriv.T))
    r_lap_y = np.kron(stiff.T, eye(nz))
    r_lap_z = np.kron(eye(8), np.kron(eye(ez), stiff.T))
    sx_rows = up8(10 * ex, 8)

    def extend(count):
        out = np.zeros((10 * count, 8 * (count + 2)))
        for elem in range(count):
            base = 8 * (elem + 1)
            out[10 * elem, base - 2] = 1.0
            for node in range(8):
                out[10 * elem + 1 + node, base + node] = 1.0
            out[10 * elem + 9, base + 9] = 1.0
        return out

    l_spec = padded(
        np.kron(eye(ex), vecs.T) @ extend(ex) @ face_sum(ex + 2), sx_rows, ring_x
    )
    ext_y = vecs.T @ extend(1) @ face_sum(3)
    ext_z = np.kron(eye(ez), vecs.T) @ extend(ez)[:, 8:-8] @ sum_z
    slanes = up8(100 * ez, 128)
    r_spec = padded(np.kron(ext_y, ext_z).T, 3 * tile, slanes)
    inner = vecs[1:9]
    r_fix = padded(np.kron(inner, sum_z @ np.kron(eye(ez), inner)).T, slanes, tile)
    l_fix = padded(face_sum(ex) @ np.kron(eye(ex), inner), 8 * ex, sx_rows)

    def field(rows, lanes):
        return np.broadcast_to(rows, (rows.shape[0], lanes.shape[-1])) * lanes

    def lane_of(y_part, z_part, reps=1):
        return np.tile((y_part[:, None] * z_part[None, :]).reshape(1, -1), (1, reps))

    ones = np.ones
    zsel = np.repeat(np.arange(ez), 12)
    g_tab = np.stack(
        [
            padded(
                field(np.tile(gauss, ex)[:, None], lane_of(gauss, np.tile(gauss, ez))),
                gx_rows,
                glanes,
            ),
            padded(field(ones((gx_rows, 1)), lane_of(ones(12), zsel)), gx_rows, glanes),
            padded(
                field((np.arange(gx_rows) // 12)[:, None], ones((1, glanes))),
                gx_rows,
                glanes,
            ),
        ]
    )
    zspec = np.repeat(np.arange(ez), 10)
    xspec = np.minimum(np.arange(sx_rows) // 10, ex - 1)[:, None]
    s_tab = np.stack(
        [
            padded(field(np.tile(lam, ex)[:, None], ones((1, slanes))), sx_rows, slanes, 1.0),
            padded(field(ones((sx_rows, 1)), lane_of(lam, ones(10 * ez))), sx_rows, slanes, 1.0),
            padded(
                field(ones((sx_rows, 1)), lane_of(ones(10), np.tile(lam, ez))),
                sx_rows,
                slanes,
                1.0,
            ),
            padded(field(ones((sx_rows, 1)), lane_of(ones(10), zspec)), sx_rows, slanes),
            field(xspec, ones((1, slanes))),
        ]
    )
    wi = np.tile(gll, ex + 2)[:, None]
    wz = np.tile(gll, ez)
    one_x = ones((ring_x, 1))
    wj_l = lane_of(gll, ones(nz), ey + 2)
    wk_l = lane_of(ones(8), wz, ey + 2)

    def inside(count):
        out = ones(8 * count)
        for face in range(1, count):
            out[8 * face - 1 : 8 * face + 1] = 2.0
        return np.concatenate([out[-8:], out, out[:8]])

    many = lane_of(inside(ey), ones(nz))
    znode = np.arange(nz)
    zlow = ((znode % 8 == 7) & (znode < nz - 1)).astype(np.float64)
    zhigh = ((znode % 8 == 0) & (znode > 0)).astype(np.float64)
    xs = np.zeros(ring_x)
    xh = np.zeros(ring_x)
    for edge in (8, 8 * (ex + 1)):
        xs[edge - 1] = 1.0
        xh[edge] = 1.0
    ys = np.zeros(8 * (ey + 2))
    yh = np.zeros(8 * (ey + 2))
    for edge in (8, 8 * (ey + 1)):
        ys[edge - 1] = 1.0
        yh[edge] = 1.0
    full = lane_of(ones(8), ones(nz), ey + 2)
    ring = np.stack(
        [
            field(one_x, wj_l * wk_l),
            field(wi, wk_l),
            field(wi, wj_l),
            field(wi, wj_l * wk_l),
            field(inside(ex)[:, None], many),
            field(one_x, lane_of(ones(8), np.repeat(np.arange(ez), 8), ey + 2)),
            field(one_x, wk_l),
            field(one_x, lane_of(ones(8), zlow, ey + 2)),
            field(one_x, lane_of(ones(8), zhigh, ey + 2)),
            field(xs[:, None], full),
            field(xh[:, None], full),
            field(one_x, lane_of(ys, ones(nz))),
            field(one_x, lane_of(yh, ones(nz))),
        ]
    )
    own = 8 * ex
    x_own = np.stack(
        [
            np.broadcast_to(v[:, None], (own, 128))
            for v in (
                np.tile(gll, ex),
                np.arange(own) // 8,
                face_sum(ex)[np.arange(own), np.arange(own) ^ 0] * 0.0
                + ((np.arange(own) % 8 == 7) & (np.arange(own) < own - 1)),
                ((np.arange(own) % 8 == 0) & (np.arange(own) > 0)).astype(np.float64),
            )
        ]
    )
    ynode = np.arange(8 * ey)
    y_own = np.stack(
        [
            np.broadcast_to(lane_of(v.astype(np.float64), ones(nz)), (8, 8 * ey * nz))
            for v in (
                np.tile(gll, ey),
                ynode // 8,
                (ynode % 8 == 7) & (ynode < 8 * ey - 1),
                (ynode % 8 == 0) & (ynode > 0),
            )
        ]
    )
    mats = [
        halves(m)
        for m in (
            l_in,
            r_in,
            r_back,
            l_back,
            l_div,
            l_lap,
            r_div_y,
            r_div_z,
            r_lap_y,
            r_lap_z,
            l_spec,
            r_spec,
            r_fix,
            l_fix,
        )
    ]
    tabs = [np.asarray(t, np.float32) for t in (g_tab, s_tab, ring, x_own, y_own)]
    return mats + tabs


def dot(a, b):
    return jnp.dot(a, b, preferred_element_type=F32)


def split(value):
    high = value.astype(BF16)
    return high, (value - high.astype(F32)).astype(BF16)


def times(value, table):
    high, low = split(value)
    return dot(high, table[0]) + (dot(high, table[1]) + dot(low, table[0]))


def table_times(table, value):
    high, low = split(value)
    return dot(table[0], high) + (dot(table[1], high) + dot(table[0], low))


def kernel(ex, ey, ez, n_x, n_y, *refs):
    n_tab = 24
    outer, all_ref = refs[:n_tab], refs[n_tab]
    held = refs[n_tab + 1 : 2 * n_tab + 1]
    (xs_ref, ys_ref, zs_ref, count_ref, vel_ref) = held[:5]
    (
        l_in,
        r_in,
        r_back,
        l_back,
        l_div,
        l_lap,
        r_div_y,
        r_div_z,
        r_lap_y,
        r_lap_z,
        l_spec,
        r_spec,
        r_fix,
        l_fix,
        g_tab,
        s_tab,
        ring,
        x_own,
        y_own,
    ) = held[5:]
    e_mask, e_gx, e_gy, e_col, e_row, e_draw, e_fix1, e_fix2, send, recv, load = refs[2 * n_tab + 1 :]
    nx, nz = 8 * ex, 8 * ez
    tile = 8 * nz
    lanes = ey * tile
    rows = nx + 16
    wide = lanes + 2 * tile
    mx, my = lax.axis_index("gx"), lax.axis_index("gy")

    def peer(dx, dy):
        return (lax.rem(mx + dx + n_x, n_x), lax.rem(my + dy + n_y, n_y))

    sides = [(dx, dy) for dx in (-1, 1, 0) for dy in (-1, 1, 0) if (dx, dy) != (0, 0)]

    barrier = pltpu.get_barrier_semaphore()
    for dx, dy in sides:
        pl.semaphore_signal(barrier, inc=1, device_id=peer(dx, dy), device_id_type=MESH)
    loads = [
        pltpu.make_async_copy(outer[i], held[i], load.at[i])
        for i in range(n_tab)
    ]
    for copy in loads:
        copy.start()

    def ready(*which):
        for i in which:
            loads[i].wait()


    def x_span(dx):
        if dx == 0:
            return (8, nx), 8
        return ((nx, 8), 0) if dx > 0 else ((8, 8), nx + 8)

    def y_span(dy):
        if dy == 0:
            return (tile, lanes), tile
        return ((lanes, tile), 0) if dy > 0 else ((tile, tile), lanes + tile)

    slot = [0]

    def send_one(make, dx, dy):
        index = slot[0]
        slot[0] += 1
        src, dst = make(dx, dy)
        copy = pltpu.make_async_remote_copy(
            src_ref=src,
            dst_ref=dst,
            send_sem=send.at[index],
            recv_sem=recv.at[index],
            device_id=peer(dx, dy),
            device_id_type=MESH,
        )
        copy.start()
        return copy

    def block(ref):
        def make(dx, dy):
            (r0, rn), rd = x_span(dx)
            (c0, cn), cd = y_span(dy)
            lead = (slice(None),) * (len(ref.shape) - 2)
            return (
                ref.at[lead + (pl.ds(r0, rn), pl.ds(c0, cn))],
                ref.at[lead + (pl.ds(rd, rn), pl.ds(cd, cn))],
            )

        return make

    def group(dx):
        return 0 if dx == 0 else (1 if dx > 0 else 2)

    def mask_part(dx, dy):
        (c0, cn), cd = y_span(dy)
        return (
            e_mask.at[0, pl.ds(0, 1), pl.ds(c0, cn)],
            e_mask.at[group(dx), pl.ds(0, 1), pl.ds(cd, cn)],
        )

    def row_part(dx, dy):
        (c0, cn), cd = y_span(dy)
        return e_row.at[0, :, pl.ds(c0, cn)], e_row.at[group(dx), :, pl.ds(cd, cn)]

    def col_part(dx, dy):
        (r0, rn), rd = x_span(dx)
        return (
            e_col.at[0, pl.ds(r0, rn), :],
            e_col.at[group(dy), pl.ds(rd, rn), :],
        )

    def last_part(dx, dy):
        (c0, cn), cd = y_span(dy)
        if dx == 0:
            r0, rn, rd = 8, nx, 8
        else:
            r0, rn, rd = (nx + 7, 1, 7) if dx > 0 else (8, 1, nx + 8)
        return (
            e_fix2.at[pl.ds(r0, rn), pl.ds(c0, cn)],
            e_fix2.at[pl.ds(rd, rn), pl.ds(cd, cn)],
        )

    def send_all(make):
        return [send_one(make, dx, dy) for dx, dy in sides]

    def only_x(dx, dy):
        (r0, rn), rd = x_span(dx)
        return e_gx.at[:, pl.ds(r0, rn), :], e_gx.at[:, pl.ds(rd, rn), :]

    def only_y(dx, dy):
        (c0, cn), cd = y_span(dy)
        return (
            e_gy.at[:, pl.ds(0, 1), pl.ds(c0, cn)],
            e_gy.at[:, pl.ds(0, 1), pl.ds(cd, cn)],
        )

    def pick(which, sizes, count):
        out = jnp.where(which > 0.5, sizes[1], sizes[0]) if count > 1 else sizes[0]
        for elem in range(2, count):
            out = jnp.where(which > elem - 0.5, sizes[elem], out)
        return out

    ready(*range(5), 21, 22, 23)
    ny = 8 * ey
    xs = [xs_ref[e] for e in range(ex)]
    ys = [ys_ref[e] for e in range(ey)]
    zs = [zs_ref[e] for e in range(ez)]
    count = count_ref[0, 0].astype(F32)

    vel = jnp.concatenate(
        [
            jnp.concatenate(
                [vel_ref[pl.ds(c * ny + y, nx, stride=3 * ny), :] for y in range(ny)], axis=1
            )
            for c in range(3)
        ],
        axis=0,
    )
    vel = [vel[c * nx : (c + 1) * nx] for c in range(3)]
    own_x, own_y = pl.ds(8, nx), pl.ds(tile, lanes)
    mask_own = jnp.where(ring[5, own_x, own_y] < count, 1.0, 0.0)
    e_mask[0, :, own_y] = mask_own[:8]
    hx = pick(x_own[1], xs, ex)
    part = hx * x_own[0]
    e_gx[0, 8 : 8 + nx, :] = hx
    sum_x = part + x_own[2] * pltpu.roll(part, nx - 1, 0) + x_own[3] * pltpu.roll(part, 1, 0)
    e_gx[1, 8 : 8 + nx, :] = sum_x
    hx_own = hx
    hy = pick(y_own[1], ys, ey)
    part = hy * y_own[0]
    e_gy[0, :, tile : tile + lanes] = hy
    sum_y = (
        part + y_own[2] * pltpu.roll(part, lanes - nz, 1) + y_own[3] * pltpu.roll(part, nz, 1)
    )
    e_gy[1, :, tile : tile + lanes] = sum_y
    hy_own = hy

    rows_g = g_tab.shape[1]
    wide_g = g_tab.shape[2]
    ready(5, 6, 19)
    at_x = table_times(l_in, jnp.concatenate(vel, axis=0))
    by_tile = [at_x[:, f * tile : (f + 1) * tile] for f in range(ey)]
    both = times(jnp.concatenate(by_tile, axis=0), r_in.at[:, :, :wide_g])
    others = times(
        jnp.concatenate([t[: 3 * rows_g] for t in by_tile], axis=0), r_in.at[:, :, wide_g:]
    )

    layer_g = g_tab[1]
    alpha = g_tab[0] * jnp.where(layer_g < count, 0.25, 0.0)
    hx_g = pick(g_tab[2], xs, ex)
    hz_g = pick(layer_g, zs, ez)
    pieces = []
    for f in range(ey):
        base = f * 6 * rows_g
        u = [both[base + c * rows_g : base + (c + 1) * rows_g] for c in range(3)]
        s0 = u[0] * (alpha * hz_g * ys[f])
        s1 = u[1] * (alpha * hz_g * hx_g)
        s2 = u[2] * (alpha * hx_g * ys[f])
        for c in range(3):
            at = f * 3 * rows_g + c * rows_g
            in_x = both[base + (3 + c) * rows_g : base + (4 + c) * rows_g]
            in_y = others[at : at + rows_g, :wide_g]
            in_z = others[at : at + rows_g, wide_g:]
            pieces.append(s0 * in_x + s1 * in_y + s2 * in_z)
    ready(7, 8)
    back = times(jnp.concatenate(pieces, axis=0), r_back)
    back = jnp.concatenate(
        [back[f * 3 * rows_g : (f + 1) * 3 * rows_g] for f in range(ey)], axis=1
    )
    weak = table_times(l_back, back)
    in_low = jnp.concatenate([y_own[2]] * (3 * nx // 8), axis=0)
    in_high = jnp.concatenate([y_own[3]] * (3 * nx // 8), axis=0)

    def inner_faces(value, low, high):
        return (
            value
            + low * pltpu.roll(value, lanes - nz, 1)
            + high * pltpu.roll(value, nz, 1)
        )

    weak = inner_faces(weak, in_low, in_high)
    weak = [weak[c * nx : (c + 1) * nx] for c in range(3)]

    def on_rows(piece, width):
        return jnp.concatenate([piece] * (width // 128), axis=1)

    def on_lanes(piece, depth):
        return jnp.concatenate([piece] * (depth // 8), axis=0)

    def pair_lanes(value, low, high):
        width = value.shape[1]
        return value + low * pltpu.roll(value, width - 1, 1) + high * pltpu.roll(value, 1, 1)

    def stacked(value, tiles):
        return jnp.concatenate(
            [value[:, t * tile : (t + 1) * tile] for t in range(tiles)], axis=0
        )

    def unstacked(value, tiles):
        depth = value.shape[0] // tiles
        return jnp.concatenate([value[t * depth : (t + 1) * depth] for t in range(tiles)], axis=1)

    ready(9, 11, 12)
    hx_o, hy_o = on_rows(hx_own, lanes), on_lanes(hy_own, nx)
    hz_o = pick(ring[5, own_x, own_y], zs, ez)
    sum_z = pair_lanes(
        mask_own * hz_o * ring[6, own_x, own_y], ring[7, own_x, own_y], ring[8, own_x, own_y]
    )
    lumped = on_rows(sum_x, lanes) * on_lanes(sum_y, nx) * sum_z * 0.125
    row_at = lax.broadcasted_iota(jnp.int32, (nx, lanes), 0)
    lane_at = lax.broadcasted_iota(jnp.int32, (nx, lanes), 1)
    within = (row_at > 0) & (row_at < nx - 1) & (lane_at >= nz) & (lane_at < lanes - nz)
    rate = jnp.where(within, time_step / jnp.where(lumped > 0.0, lumped, 1.0), 0.0)
    known = [(vel[c] - weak[c] * rate) * mask_own for c in range(3)]
    quarter = (-0.25 * mask_own) * ring[3, own_x, own_y]
    tall = jnp.concatenate([known[0], jnp.zeros((16, lanes), F32)], axis=0)
    e_draw[own_x, own_y] = (
        quarter * hy_o * hz_o * table_times(l_div, tall)[:nx]
        + quarter * hx_o * hz_o * unstacked(times(stacked(known[1], ey), r_div_y), ey)
        + quarter * hx_o * hy_o * unstacked(times(stacked(known[2], ey), r_div_z), ey)
    )
    e_row[0, :, own_y] = jnp.concatenate(
        [w[:1] for w in weak] + [w[nx - 1 :] for w in weak] + [weak[0][:2]], axis=0
    )
    e_col[0, own_x, :] = jnp.concatenate(
        [w[:, :nz] for w in weak] + [w[:, lanes - nz :] for w in weak] + [weak[0][:, : tile - 6 * nz]],
        axis=1,
    )

    pl.semaphore_wait(barrier, len(sides))
    first = send_all(mask_part)
    first += [send_one(only_x, 1, 0), send_one(only_x, -1, 0)]
    first += [send_one(only_y, 0, 1), send_one(only_y, 0, -1)]
    second = send_all(col_part) + send_all(row_part) + send_all(block(e_draw))

    def cross(value):
        value = (
            value
            + ring[9] * pltpu.roll(value, rows - 1, 0)
            + ring[10] * pltpu.roll(value, 1, 0)
        )
        return (
            value
            + ring[11] * pltpu.roll(value, wide - nz, 1)
            + ring[12] * pltpu.roll(value, nz, 1)
        )

    def pair_z(value):
        return pair_lanes(value, ring[7], ring[8])

    ready(10, *range(13, 19), 20)
    for copy in first:
        copy.wait_recv()
    mask = jnp.concatenate(
        [jnp.broadcast_to(e_mask[g, 0:1, :], (n, wide)) for g, n in ((1, 8), (0, nx), (2, 8))],
        axis=0,
    )
    hz_r = pick(ring[5], zs, ez)

    hx_r = on_rows(e_gx[0], wide)
    hy_r = jnp.broadcast_to(e_gy[0, 0:1, :], (rows, wide))
    sum_y = jnp.broadcast_to(e_gy[1, 0:1, :], (rows, wide))
    lumped = cross(on_rows(e_gx[1], wide) * sum_y * pair_z(mask * hz_r * ring[6]) * 0.125)
    inv_lumped = time_step / jnp.where(lumped > 0.0, lumped, 1.0)
    mult = cross(ring[4] * pair_z(mask))
    inv_mult = mask / jnp.maximum(mult, 1.0)
    quarter = (-0.25 * mask) * ring[3]
    c_x, c_y, c_z = quarter * hy_r * hz_r, quarter * hx_r * hz_r, quarter * hx_r * hy_r
    k_x = mask * (hy_r * hz_r / (2.0 * hx_r)) * ring[0]
    k_y = mask * (hx_r * hz_r / (2.0 * hy_r)) * ring[1]
    k_z = mask * (hx_r * hy_r / (2.0 * hz_r)) * ring[2]
    layer_s = s_tab[3]
    hx_s = pick(s_tab[4], xs, ex)
    hz_s = pick(layer_s, zs, ez)
    keep = jnp.where(layer_s < count, 1.0, 0.0)
    scales = []
    for f in range(ey):
        denom = ys[f] * hz_s / (2.0 * hx_s) * s_tab[0]
        denom = denom + hx_s * hz_s / (2.0 * ys[f]) * s_tab[1]
        denom = denom + hx_s * ys[f] / (2.0 * hz_s) * s_tab[2]
        scales.append(keep / denom)
    scale = jnp.concatenate(scales, axis=0)
    rows_s = s_tab.shape[1]

    def schwarz(raw, target, make):
        spec_x = table_times(l_spec, raw)
        spec_x = jnp.concatenate(
            [spec_x[:, f * tile : (f + 3) * tile] for f in range(ey)], axis=0
        )
        spec = times(spec_x, r_spec) * scale
        fixed = times(spec, r_fix)
        fixed = jnp.concatenate(
            [fixed[f * rows_s : (f + 1) * rows_s] for f in range(ey)], axis=1
        )
        fixed = table_times(l_fix, fixed)
        fixed = inner_faces(fixed, in_low[:nx], in_high[:nx])
        target[8 : 8 + nx, tile : tile + lanes] = fixed
        return send_all(make)

    for copy in second:
        copy.wait_recv()
    down, up = 3 * nz, 6 * nz
    low_col = e_col[0, :, :down] + e_col[1, :, down:up]
    high_col = e_col[0, :, down:up] + e_col[2, :, :down]

    def cross_rows(value):
        width = value.shape[1]
        return (
            value
            + ring[9, :, :width] * pltpu.roll(value, rows - 1, 0)
            + ring[10, :, :width] * pltpu.roll(value, 1, 0)
        )

    cols = cross_rows(jnp.concatenate([low_col, high_col, jnp.zeros((rows, tile - up), F32)], axis=1))
    edge = jnp.concatenate(
        [
            e_row[0, 0:3] + e_row[1, 3:6],
            e_row[0, 3:6] + e_row[2, 0:3],
            jnp.zeros((2, wide), F32),
        ],
        axis=0,
    )
    edge = (
        edge
        + ring[11, :8] * pltpu.roll(edge, wide - nz, 1)
        + ring[12, :8] * pltpu.roll(edge, nz, 1)
    )
    ring_row = lax.broadcasted_iota(jnp.int32, (rows, wide), 0)
    at_low = (ring_row == 7) | (ring_row == 8)
    at_high = (ring_row == nx + 7) | (ring_row == nx + 8)
    gap = jnp.zeros((rows, tile - nz), F32)
    middle = jnp.zeros((rows, lanes - 2 * nz), F32)
    change = []
    for c in range(3):
        low = cols[:, c * nz : (c + 1) * nz]
        high = cols[:, down + c * nz : down + (c + 1) * nz]
        value = jnp.concatenate([gap, low, low, middle, high, high, gap], axis=1)
        value = jnp.where(at_low, edge[c : c + 1], value)
        value = jnp.where(at_high, edge[3 + c : 4 + c], value)
        change.append(value * inv_lumped * mask)
    adv = [known[c] - change[c][8 : 8 + nx, tile : tile + lanes] for c in range(3)]
    raw = e_draw[...] - (
        c_x * table_times(l_div, change[0])
        + c_y * unstacked(times(stacked(change[1], ey + 2), r_div_y), ey + 2)
        + c_z * unstacked(times(stacked(change[2], ey + 2), r_div_z), ey + 2)
    )
    third = schwarz(raw, e_fix1, block(e_fix1))
    for c in range(3):
        all_ref[c * nx : (c + 1) * nx, :] = adv[c]
    for copy in third:
        copy.wait_recv()
    press = cross(e_fix1[...]) * inv_mult
    by_y = stacked(press, ey + 2)
    raw = raw - (
        k_x * table_times(l_lap, press)
        + k_y * unstacked(times(by_y, r_lap_y), ey + 2)
        + k_z * unstacked(times(by_y, r_lap_z), ey + 2)
    )
    fourth = schwarz(raw, e_fix2, last_part)
    for copy in fourth:
        copy.wait_recv()
    press = press + cross(e_fix2[...]) * inv_mult
    all_ref[3 * nx :, :] = press[8 : 8 + nx, tile : tile + lanes]
    for copy in first + second + third + fourth:
        copy.wait_send()


def lay_out(nx, ny, nz, all_ref, adv_ref, press_ref):
    for c in range(3):
        own = all_ref[c * nx : (c + 1) * nx, :]
        for y in range(ny):
            adv_ref[pl.ds(c * ny + y, nx, stride=3 * ny), :] = own[:, y * nz : (y + 1) * nz]
    own = all_ref[3 * nx :, :]
    for y in range(ny):
        press_ref[pl.ds(y, nx, stride=ny), :] = own[:, y * nz : (y + 1) * nz]


def local(n_x, n_y, velocity, x_sizes, y_sizes, z_sizes, layer_counts):
    ex, ey, ez = x_sizes.shape[0], y_sizes.shape[0], z_sizes.shape[0]
    nx, ny, nz = 8 * ex, 8 * ey, 8 * ez
    tile = 8 * nz
    lanes = ny * nz
    rows, wide = nx + 16, lanes + 2 * tile
    vel = velocity.transpose(0, 2, 1, 3).reshape(3 * nx * ny, nz)
    consts = [jnp.asarray(c) for c in constants(ex, ey, ez)]
    vmem = pl.BlockSpec(memory_space=pltpu.VMEM)
    copies = 6 * 8 + 4
    scalars = (x_sizes, y_sizes, z_sizes, layer_counts)
    tables_in = (vel, *consts)
    both = pl.pallas_call(
        functools.partial(kernel, ex, ey, ez, n_x, n_y),
        out_shape=jax.ShapeDtypeStruct((4 * nx, lanes), F32),
        in_specs=[pl.BlockSpec(memory_space=pl.ANY)] * (4 + len(tables_in)),
        out_specs=vmem,
        scratch_shapes=[pltpu.SMEM(a.shape, a.dtype) for a in scalars]
        + [pltpu.VMEM(a.shape, a.dtype) for a in tables_in]
        + [
            pltpu.VMEM((3, 8, wide), F32),
            pltpu.VMEM((2, rows, 128), F32),
            pltpu.VMEM((2, 8, wide), F32),
            pltpu.VMEM((3, rows, tile), F32),
            pltpu.VMEM((3, 8, wide), F32),
            pltpu.VMEM((rows, wide), F32),
            pltpu.VMEM((rows, wide), F32),
            pltpu.VMEM((rows, wide), F32),
            pltpu.SemaphoreType.DMA((copies,)),
            pltpu.SemaphoreType.DMA((copies,)),
            pltpu.SemaphoreType.DMA((4 + len(tables_in),)),
        ],
        compiler_params=pltpu.CompilerParams(collective_id=0, has_side_effects=True),
        name="sem_step",
    )(*scalars, *tables_in)
    adv, press = pl.pallas_call(
        functools.partial(lay_out, nx, ny, nz),
        out_shape=(
            jax.ShapeDtypeStruct((3 * nx * ny, nz), F32),
            jax.ShapeDtypeStruct((nx * ny, nz), F32),
        ),
        in_specs=[vmem],
        out_specs=(vmem, vmem),
        name="lay_out",
    )(both)
    advected = adv.reshape(nx, 3, ny, nz).transpose(0, 2, 1, 3)
    return advected, press.reshape(nx, ny, nz)


def solution(mesh):
    in_specs = (P("gx", "gy", None, None), P("gx"), P("gy"), P(), P("gx", "gy"))
    out_specs = (P("gx", "gy", None, None), P("gx", "gy", None))
    body = functools.partial(local, mesh.shape["gx"], mesh.shape["gy"])
    return jax.shard_map(body, mesh=mesh, in_specs=in_specs, out_specs=out_specs, check_vma=False)
```

```python
import functools
import math

import jax
import jax.numpy as jnp
import numpy as np
from jax import lax
from jax.experimental import pallas as pl
from jax.experimental.pallas import tpu as pltpu
from jax.sharding import PartitionSpec as P

SWEEPS = 2
time_step = 0.005
MESH = pl.DeviceIdType.MESH
F32 = jnp.float32
BF16 = jnp.bfloat16


def legendre_value(order, point):
    previous = 1.0
    current = point
    for degree in range(2, order + 1):
        previous, current = (
            current,
            ((2 * degree - 1) * point * current - (degree - 1) * previous) / degree,
        )
    return current


def legendre_pair(order, point):
    previous = 1.0
    current = point
    for degree in range(2, order + 1):
        previous, current = (
            current,
            ((2 * degree - 1) * point * current - (degree - 1) * previous) / degree,
        )
    slope = order * (point * current - previous) / (point * point - 1.0)
    return (current, slope)


def tables():
    inner_points = []
    for index in range(1, 7):
        point = -math.cos(math.pi * index / 7.0)
        for newton in range(60):
            value, slope = legendre_pair(7, point)
            curvature = (2.0 * point * slope - 56.0 * value) / (1.0 - point * point)
            point = point - slope / curvature
        inner_points.append(point)
    gll_points = [-1.0] + inner_points + [1.0]
    gll_weights = [2.0 / (56.0 * legendre_value(7, point) ** 2) for point in gll_points]
    barycentric = []
    for first in range(8):
        product = 1.0
        for second in range(8):
            if second != first:
                product = product * (gll_points[first] - gll_points[second])
        barycentric.append(1.0 / product)
    derivative = [[0.0] * 8 for first in range(8)]
    for first in range(8):
        total = 0.0
        for second in range(8):
            if second != first:
                entry = (
                    barycentric[second]
                    / barycentric[first]
                    / (gll_points[first] - gll_points[second])
                )
                derivative[first][second] = entry
                total = total + entry
        derivative[first][first] = -total
    gauss_points = []
    gauss_weights = []
    for index in range(1, 13):
        point = -math.cos(math.pi * (index - 0.25) / 12.5)
        for newton in range(60):
            value, slope = legendre_pair(12, point)
            point = point - value / slope
        value, slope = legendre_pair(12, point)
        gauss_points.append(point)
        gauss_weights.append(2.0 / ((1.0 - point * point) * slope * slope))
    interpolate = []
    for gauss in gauss_points:
        fraction = [barycentric[node] / (gauss - gll_points[node]) for node in range(8)]
        total = sum(fraction)
        interpolate.append([entry / total for entry in fraction])
    stiffness = [
        [
            sum(
                (
                    derivative[inner][first] * gll_weights[inner] * derivative[inner][second]
                    for inner in range(8)
                )
            )
            for second in range(8)
        ]
        for first in range(8)
    ]
    glob_stiff = [[0.0] * 22 for first in range(22)]
    glob_mass = [0.0] * 22
    for offset in (0, 7, 14):
        for first in range(8):
            glob_mass[offset + first] = glob_mass[offset + first] + gll_weights[first]
            for second in range(8):
                glob_stiff[offset + first][offset + second] = (
                    glob_stiff[offset + first][offset + second] + stiffness[first][second]
                )
    inv_root = [1.0 / math.sqrt(glob_mass[6 + first]) for first in range(10)]
    matrix = [
        [
            inv_root[first] * glob_stiff[6 + first][6 + second] * inv_root[second]
            for second in range(10)
        ]
        for first in range(10)
    ]
    rotation = [[1.0 if first == second else 0.0 for second in range(10)] for first in range(10)]
    for sweep in range(20):
        for first in range(10):
            for second in range(first + 1, 10):
                angle = 0.5 * math.atan2(
                    2.0 * matrix[first][second], matrix[second][second] - matrix[first][first]
                )
                cosine = math.cos(angle)
                sine = math.sin(angle)
                for other in range(10):
                    left_val = matrix[other][first]
                    right_val = matrix[other][second]
                    matrix[other][first] = cosine * left_val - sine * right_val
                    matrix[other][second] = sine * left_val + cosine * right_val
                    left_val = rotation[other][first]
                    right_val = rotation[other][second]
                    rotation[other][first] = cosine * left_val - sine * right_val
                    rotation[other][second] = sine * left_val + cosine * right_val
                for other in range(10):
                    upper_val = matrix[first][other]
                    lower_val = matrix[second][other]
                    matrix[first][other] = cosine * upper_val - sine * lower_val
                    matrix[second][other] = sine * upper_val + cosine * lower_val
    eigen_values = [matrix[first][first] for first in range(10)]
    vectors = [
        [inv_root[first] * rotation[first][second] for second in range(10)] for first in range(10)
    ]
    return tuple(
        np.asarray(table, dtype=np.float64)
        for table in (
            derivative,
            gll_weights,
            interpolate,
            gauss_weights,
            stiffness,
            vectors,
            eigen_values,
        )
    )


def halves(matrix):
    matrix = np.asarray(matrix, np.float32)
    high = matrix.astype(BF16)
    low = (matrix - high.astype(np.float32)).astype(BF16)
    return np.stack([high, low])


def padded(matrix, rows, cols, fill=0.0):
    out = np.full((rows, cols), fill, np.float64)
    out[: matrix.shape[0], : matrix.shape[1]] = matrix
    return out


def face_sum(count):
    out = np.eye(8 * count)
    for face in range(1, count):
        out[8 * face - 1, 8 * face] = 1.0
        out[8 * face, 8 * face - 1] = 1.0
    return out


def up8(value, step):
    return -(-value // step) * step


def constants(ex, ey, ez):
    deriv, gll, interp, gauss, stiff, vecs, lam = tables()
    eye = np.eye
    gx_rows = up8(12 * ex, 8)
    nz = 8 * ez
    tile = 8 * nz
    glanes = up8(144 * ez, 128)
    int_d = interp @ deriv
    sum_z = face_sum(ez)
    jx = padded(np.kron(eye(ex), interp), gx_rows, 8 * ex)
    dx = padded(np.kron(eye(ex), int_d), gx_rows, 8 * ex)
    l_in = np.concatenate([np.kron(eye(3), jx), np.kron(eye(3), dx)])
    jz = np.kron(eye(ez), interp)
    dz = np.kron(eye(ez), int_d)
    r_in = np.concatenate(
        [
            padded(np.kron(a, b).T, tile, glanes)
            for a, b in ((interp, jz), (int_d, jz), (interp, dz))
        ],
        axis=1,
    )
    r_back = padded(np.kron(interp, jz @ sum_z.T), glanes, tile)
    l_back = np.kron(eye(3), face_sum(ex) @ jx.T)
    ring_x = 8 * (ex + 2)
    l_div = np.kron(eye(ex + 2), deriv)
    l_lap = np.kron(eye(ex + 2), stiff)
    r_div_y = np.kron(deriv.T, eye(nz))
    r_div_z = np.kron(eye(8), np.kron(eye(ez), deriv.T))
    r_lap_y = np.kron(stiff.T, eye(nz))
    r_lap_z = np.kron(eye(8), np.kron(eye(ez), stiff.T))
    sx_rows = up8(10 * ex, 8)

    def extend(count):
        out = np.zeros((10 * count, 8 * (count + 2)))
        for elem in range(count):
            base = 8 * (elem + 1)
            out[10 * elem, base - 2] = 1.0
            for node in range(8):
                out[10 * elem + 1 + node, base + node] = 1.0
            out[10 * elem + 9, base + 9] = 1.0
        return out

    l_spec = padded(
        np.kron(eye(ex), vecs.T) @ extend(ex) @ face_sum(ex + 2), sx_rows, ring_x
    )
    ext_y = vecs.T @ extend(1) @ face_sum(3)
    ext_z = np.kron(eye(ez), vecs.T) @ extend(ez)[:, 8:-8] @ sum_z
    slanes = up8(100 * ez, 128)
    r_spec = padded(np.kron(ext_y, ext_z).T, 3 * tile, slanes)
    inner = vecs[1:9]
    r_fix = padded(np.kron(inner, sum_z @ np.kron(eye(ez), inner)).T, slanes, tile)
    l_fix = padded(face_sum(ex) @ np.kron(eye(ex), inner), 8 * ex, sx_rows)

    def field(rows, lanes):
        return np.broadcast_to(rows, (rows.shape[0], lanes.shape[-1])) * lanes

    def lane_of(y_part, z_part, reps=1):
        return np.tile((y_part[:, None] * z_part[None, :]).reshape(1, -1), (1, reps))

    ones = np.ones
    zsel = np.repeat(np.arange(ez), 12)
    g_tab = np.stack(
        [
            padded(
                field(np.tile(gauss, ex)[:, None], lane_of(gauss, np.tile(gauss, ez))),
                gx_rows,
                glanes,
            ),
            padded(field(ones((gx_rows, 1)), lane_of(ones(12), zsel)), gx_rows, glanes),
            padded(
                field((np.arange(gx_rows) // 12)[:, None], ones((1, glanes))),
                gx_rows,
                glanes,
            ),
        ]
    )
    zspec = np.repeat(np.arange(ez), 10)
    xspec = np.minimum(np.arange(sx_rows) // 10, ex - 1)[:, None]
    s_tab = np.stack(
        [
            padded(field(np.tile(lam, ex)[:, None], ones((1, slanes))), sx_rows, slanes, 1.0),
            padded(field(ones((sx_rows, 1)), lane_of(lam, ones(10 * ez))), sx_rows, slanes, 1.0),
            padded(
                field(ones((sx_rows, 1)), lane_of(ones(10), np.tile(lam, ez))),
                sx_rows,
                slanes,
                1.0,
            ),
            padded(field(ones((sx_rows, 1)), lane_of(ones(10), zspec)), sx_rows, slanes),
            field(xspec, ones((1, slanes))),
        ]
    )
    wi = np.tile(gll, ex + 2)[:, None]
    wz = np.tile(gll, ez)
    one_x = ones((ring_x, 1))
    wj_l = lane_of(gll, ones(nz), ey + 2)
    wk_l = lane_of(ones(8), wz, ey + 2)

    def inside(count):
        out = ones(8 * count)
        for face in range(1, count):
            out[8 * face - 1 : 8 * face + 1] = 2.0
        return np.concatenate([out[-8:], out, out[:8]])

    many = lane_of(inside(ey), ones(nz))
    znode = np.arange(nz)
    zlow = ((znode % 8 == 7) & (znode < nz - 1)).astype(np.float64)
    zhigh = ((znode % 8 == 0) & (znode > 0)).astype(np.float64)
    xs = np.zeros(ring_x)
    xh = np.zeros(ring_x)
    for edge in (8, 8 * (ex + 1)):
        xs[edge - 1] = 1.0
        xh[edge] = 1.0
    ys = np.zeros(8 * (ey + 2))
    yh = np.zeros(8 * (ey + 2))
    for edge in (8, 8 * (ey + 1)):
        ys[edge - 1] = 1.0
        yh[edge] = 1.0
    full = lane_of(ones(8), ones(nz), ey + 2)
    ring = np.stack(
        [
            field(one_x, wj_l * wk_l),
            field(wi, wk_l),
            field(wi, wj_l),
            field(wi, wj_l * wk_l),
            field(inside(ex)[:, None], many),
            field(one_x, lane_of(ones(8), np.repeat(np.arange(ez), 8), ey + 2)),
            field(one_x, wk_l),
            field(one_x, lane_of(ones(8), zlow, ey + 2)),
            field(one_x, lane_of(ones(8), zhigh, ey + 2)),
            field(xs[:, None], full),
            field(xh[:, None], full),
            field(one_x, lane_of(ys, ones(nz))),
            field(one_x, lane_of(yh, ones(nz))),
        ]
    )
    own = 8 * ex
    x_own = np.stack(
        [
            np.broadcast_to(v[:, None], (own, 128))
            for v in (
                np.tile(gll, ex),
                np.arange(own) // 8,
                face_sum(ex)[np.arange(own), np.arange(own) ^ 0] * 0.0
                + ((np.arange(own) % 8 == 7) & (np.arange(own) < own - 1)),
                ((np.arange(own) % 8 == 0) & (np.arange(own) > 0)).astype(np.float64),
            )
        ]
    )
    ynode = np.arange(8 * ey)
    y_own = np.stack(
        [
            np.broadcast_to(lane_of(v.astype(np.float64), ones(nz)), (8, 8 * ey * nz))
            for v in (
                np.tile(gll, ey),
                ynode // 8,
                (ynode % 8 == 7) & (ynode < 8 * ey - 1),
                (ynode % 8 == 0) & (ynode > 0),
            )
        ]
    )
    mats = [
        halves(m)
        for m in (
            l_in,
            r_in,
            r_back,
            l_back,
            l_div,
            l_lap,
            r_div_y,
            r_div_z,
            r_lap_y,
            r_lap_z,
            l_spec,
            r_spec,
            r_fix,
            l_fix,
        )
    ]
    tabs = [np.asarray(t, np.float32) for t in (g_tab, s_tab, ring, x_own, y_own)]
    return mats + tabs


def dot(a, b):
    return jnp.dot(a, b, preferred_element_type=F32)


def split(value):
    high = value.astype(BF16)
    return high, (value - high.astype(F32)).astype(BF16)


def times(value, table):
    high, low = split(value)
    return dot(high, table[0]) + (dot(high, table[1]) + dot(low, table[0]))


def table_times(table, value):
    high, low = split(value)
    return dot(table[0], high) + (dot(table[1], high) + dot(table[0], low))


def kernel(ex, ey, ez, n_x, n_y, *refs):
    n_tab = 24
    outer, all_ref = refs[:n_tab], refs[n_tab]
    held = refs[n_tab + 1 : 2 * n_tab + 1]
    (xs_ref, ys_ref, zs_ref, count_ref, vel_ref) = held[:5]
    (
        l_in,
        r_in,
        r_back,
        l_back,
        l_div,
        l_lap,
        r_div_y,
        r_div_z,
        r_lap_y,
        r_lap_z,
        l_spec,
        r_spec,
        r_fix,
        l_fix,
        g_tab,
        s_tab,
        ring,
        x_own,
        y_own,
    ) = held[5:]
    e_mask, e_gx, e_gy, e_col, e_row, e_draw, e_fix1, e_fix2, send, recv, load = refs[2 * n_tab + 1 :]
    nx, nz = 8 * ex, 8 * ez
    tile = 8 * nz
    lanes = ey * tile
    rows = nx + 16
    wide = lanes + 2 * tile
    mx, my = lax.axis_index("gx"), lax.axis_index("gy")

    def peer(dx, dy):
        return (lax.rem(mx + dx + n_x, n_x), lax.rem(my + dy + n_y, n_y))

    sides = [(-1, -1), (-1, 1), (1, -1), (1, 1), (0, -1), (0, 1), (-1, 0), (1, 0)]

    barrier = pltpu.get_barrier_semaphore()
    for dx, dy in sides:
        pl.semaphore_signal(barrier, inc=1, device_id=peer(dx, dy), device_id_type=MESH)
    loads = [
        pltpu.make_async_copy(outer[i], held[i], load.at[i])
        for i in range(n_tab)
    ]
    for copy in loads:
        copy.start()

    def ready(*which):
        for i in which:
            loads[i].wait()


    def x_span(dx):
        if dx == 0:
            return (8, nx), 8
        return ((nx, 8), 0) if dx > 0 else ((8, 8), nx + 8)

    def y_span(dy):
        if dy == 0:
            return (tile, lanes), tile
        return ((lanes, tile), 0) if dy > 0 else ((tile, tile), lanes + tile)

    slot = [0]

    def send_one(make, dx, dy):
        index = slot[0]
        slot[0] += 1
        src, dst = make(dx, dy)
        copy = pltpu.make_async_remote_copy(
            src_ref=src,
            dst_ref=dst,
            send_sem=send.at[index],
            recv_sem=recv.at[index],
            device_id=peer(dx, dy),
            device_id_type=MESH,
        )
        copy.start()
        return copy

    def block(ref):
        def make(dx, dy):
            (r0, rn), rd = x_span(dx)
            (c0, cn), cd = y_span(dy)
            lead = (slice(None),) * (len(ref.shape) - 2)
            return (
                ref.at[lead + (pl.ds(r0, rn), pl.ds(c0, cn))],
                ref.at[lead + (pl.ds(rd, rn), pl.ds(cd, cn))],
            )

        return make

    def group(dx):
        return 0 if dx == 0 else (1 if dx > 0 else 2)

    def mask_part(dx, dy):
        (c0, cn), cd = y_span(dy)
        return (
            e_mask.at[0, pl.ds(0, 1), pl.ds(c0, cn)],
            e_mask.at[group(dx), pl.ds(0, 1), pl.ds(cd, cn)],
        )

    def row_part(dx, dy):
        (c0, cn), cd = y_span(dy)
        return e_row.at[0, :, pl.ds(c0, cn)], e_row.at[group(dx), :, pl.ds(cd, cn)]

    def col_part(dx, dy):
        (r0, rn), rd = x_span(dx)
        return (
            e_col.at[0, pl.ds(r0, rn), :],
            e_col.at[group(dy), pl.ds(rd, rn), :],
        )

    def last_part(dx, dy):
        (c0, cn), cd = y_span(dy)
        if dx == 0:
            r0, rn, rd = 8, nx, 8
        else:
            r0, rn, rd = (nx + 7, 1, 7) if dx > 0 else (8, 1, nx + 8)
        return (
            e_fix2.at[pl.ds(r0, rn), pl.ds(c0, cn)],
            e_fix2.at[pl.ds(rd, rn), pl.ds(cd, cn)],
        )

    def send_all(make):
        return [send_one(make, dx, dy) for dx, dy in sides]

    def only_x(dx, dy):
        (r0, rn), rd = x_span(dx)
        return e_gx.at[:, pl.ds(r0, rn), :], e_gx.at[:, pl.ds(rd, rn), :]

    def only_y(dx, dy):
        (c0, cn), cd = y_span(dy)
        return (
            e_gy.at[:, pl.ds(0, 1), pl.ds(c0, cn)],
            e_gy.at[:, pl.ds(0, 1), pl.ds(cd, cn)],
        )

    def pick(which, sizes, count):
        out = jnp.where(which > 0.5, sizes[1], sizes[0]) if count > 1 else sizes[0]
        for elem in range(2, count):
            out = jnp.where(which > elem - 0.5, sizes[elem], out)
        return out

    ready(*range(5), 21, 22, 23)
    ny = 8 * ey
    xs = [xs_ref[e] for e in range(ex)]
    ys = [ys_ref[e] for e in range(ey)]
    zs = [zs_ref[e] for e in range(ez)]
    count = count_ref[0, 0].astype(F32)

    vel = jnp.concatenate(
        [
            jnp.concatenate(
                [vel_ref[pl.ds(c * ny + y, nx, stride=3 * ny), :] for y in range(ny)], axis=1
            )
            for c in range(3)
        ],
        axis=0,
    )
    vel = [vel[c * nx : (c + 1) * nx] for c in range(3)]
    own_x, own_y = pl.ds(8, nx), pl.ds(tile, lanes)
    mask_own = jnp.where(ring[5, own_x, own_y] < count, 1.0, 0.0)
    e_mask[0, :, own_y] = mask_own[:8]
    hx = pick(x_own[1], xs, ex)
    part = hx * x_own[0]
    e_gx[0, 8 : 8 + nx, :] = hx
    sum_x = part + x_own[2] * pltpu.roll(part, nx - 1, 0) + x_own[3] * pltpu.roll(part, 1, 0)
    e_gx[1, 8 : 8 + nx, :] = sum_x
    hx_own = hx
    hy = pick(y_own[1], ys, ey)
    part = hy * y_own[0]
    e_gy[0, :, tile : tile + lanes] = hy
    sum_y = (
        part + y_own[2] * pltpu.roll(part, lanes - nz, 1) + y_own[3] * pltpu.roll(part, nz, 1)
    )
    e_gy[1, :, tile : tile + lanes] = sum_y
    hy_own = hy

    rows_g = g_tab.shape[1]
    wide_g = g_tab.shape[2]
    ready(5, 6, 19)
    at_x = table_times(l_in, jnp.concatenate(vel, axis=0))
    by_tile = [at_x[:, f * tile : (f + 1) * tile] for f in range(ey)]
    both = times(jnp.concatenate(by_tile, axis=0), r_in.at[:, :, :wide_g])
    others = times(
        jnp.concatenate([t[: 3 * rows_g] for t in by_tile], axis=0), r_in.at[:, :, wide_g:]
    )

    layer_g = g_tab[1]
    alpha = g_tab[0] * jnp.where(layer_g < count, 0.25, 0.0)
    hx_g = pick(g_tab[2], xs, ex)
    hz_g = pick(layer_g, zs, ez)
    pieces = []
    for f in range(ey):
        base = f * 6 * rows_g
        u = [both[base + c * rows_g : base + (c + 1) * rows_g] for c in range(3)]
        s0 = u[0] * (alpha * hz_g * ys[f])
        s1 = u[1] * (alpha * hz_g * hx_g)
        s2 = u[2] * (alpha * hx_g * ys[f])
        for c in range(3):
            at = f * 3 * rows_g + c * rows_g
            in_x = both[base + (3 + c) * rows_g : base + (4 + c) * rows_g]
            in_y = others[at : at + rows_g, :wide_g]
            in_z = others[at : at + rows_g, wide_g:]
            pieces.append(s0 * in_x + s1 * in_y + s2 * in_z)
    ready(7, 8)
    back = times(jnp.concatenate(pieces, axis=0), r_back)
    back = jnp.concatenate(
        [back[f * 3 * rows_g : (f + 1) * 3 * rows_g] for f in range(ey)], axis=1
    )
    weak = table_times(l_back, back)
    in_low = jnp.concatenate([y_own[2]] * (3 * nx // 8), axis=0)
    in_high = jnp.concatenate([y_own[3]] * (3 * nx // 8), axis=0)

    def inner_faces(value, low, high):
        return (
            value
            + low * pltpu.roll(value, lanes - nz, 1)
            + high * pltpu.roll(value, nz, 1)
        )

    weak = inner_faces(weak, in_low, in_high)
    weak = [weak[c * nx : (c + 1) * nx] for c in range(3)]

    def on_rows(piece, width):
        return jnp.concatenate([piece] * (width // 128), axis=1)

    def on_lanes(piece, depth):
        return jnp.concatenate([piece] * (depth // 8), axis=0)

    def pair_lanes(value, low, high):
        width = value.shape[1]
        return value + low * pltpu.roll(value, width - 1, 1) + high * pltpu.roll(value, 1, 1)

    def stacked(value, tiles):
        return jnp.concatenate(
            [value[:, t * tile : (t + 1) * tile] for t in range(tiles)], axis=0
        )

    def unstacked(value, tiles):
        depth = value.shape[0] // tiles
        return jnp.concatenate([value[t * depth : (t + 1) * depth] for t in range(tiles)], axis=1)

    ready(9, 11, 12)
    hx_o, hy_o = on_rows(hx_own, lanes), on_lanes(hy_own, nx)
    hz_o = pick(ring[5, own_x, own_y], zs, ez)
    sum_z = pair_lanes(
        mask_own * hz_o * ring[6, own_x, own_y], ring[7, own_x, own_y], ring[8, own_x, own_y]
    )
    lumped = on_rows(sum_x, lanes) * on_lanes(sum_y, nx) * sum_z * 0.125
    row_at = lax.broadcasted_iota(jnp.int32, (nx, lanes), 0)
    lane_at = lax.broadcasted_iota(jnp.int32, (nx, lanes), 1)
    within = (row_at > 0) & (row_at < nx - 1) & (lane_at >= nz) & (lane_at < lanes - nz)
    rate = jnp.where(within, time_step / jnp.where(lumped > 0.0, lumped, 1.0), 0.0)
    known = [(vel[c] - weak[c] * rate) * mask_own for c in range(3)]
    quarter = (-0.25 * mask_own) * ring[3, own_x, own_y]
    tall = jnp.concatenate([known[0], jnp.zeros((16, lanes), F32)], axis=0)
    e_draw[own_x, own_y] = (
        quarter * hy_o * hz_o * table_times(l_div, tall)[:nx]
        + quarter * hx_o * hz_o * unstacked(times(stacked(known[1], ey), r_div_y), ey)
        + quarter * hx_o * hy_o * unstacked(times(stacked(known[2], ey), r_div_z), ey)
    )
    e_row[0, :, own_y] = jnp.concatenate(
        [w[:1] for w in weak] + [w[nx - 1 :] for w in weak] + [weak[0][:2]], axis=0
    )
    e_col[0, own_x, :] = jnp.concatenate(
        [w[:, :nz] for w in weak] + [w[:, lanes - nz :] for w in weak] + [weak[0][:, : tile - 6 * nz]],
        axis=1,
    )

    pl.semaphore_wait(barrier, len(sides))
    first = send_all(mask_part)
    first += [send_one(only_x, 1, 0), send_one(only_x, -1, 0)]
    first += [send_one(only_y, 0, 1), send_one(only_y, 0, -1)]
    second = send_all(col_part) + send_all(row_part) + send_all(block(e_draw))

    def cross(value):
        value = (
            value
            + ring[9] * pltpu.roll(value, rows - 1, 0)
            + ring[10] * pltpu.roll(value, 1, 0)
        )
        return (
            value
            + ring[11] * pltpu.roll(value, wide - nz, 1)
            + ring[12] * pltpu.roll(value, nz, 1)
        )

    def pair_z(value):
        return pair_lanes(value, ring[7], ring[8])

    ready(10, *range(13, 19), 20)
    for copy in first:
        copy.wait_recv()
    mask = jnp.concatenate(
        [jnp.broadcast_to(e_mask[g, 0:1, :], (n, wide)) for g, n in ((1, 8), (0, nx), (2, 8))],
        axis=0,
    )
    hz_r = pick(ring[5], zs, ez)

    hx_r = on_rows(e_gx[0], wide)
    hy_r = jnp.broadcast_to(e_gy[0, 0:1, :], (rows, wide))
    sum_y = jnp.broadcast_to(e_gy[1, 0:1, :], (rows, wide))
    lumped = cross(on_rows(e_gx[1], wide) * sum_y * pair_z(mask * hz_r * ring[6]) * 0.125)
    inv_lumped = time_step / jnp.where(lumped > 0.0, lumped, 1.0)
    mult = cross(ring[4] * pair_z(mask))
    inv_mult = mask / jnp.maximum(mult, 1.0)
    quarter = (-0.25 * mask) * ring[3]
    c_x, c_y, c_z = quarter * hy_r * hz_r, quarter * hx_r * hz_r, quarter * hx_r * hy_r
    k_x = mask * (hy_r * hz_r / (2.0 * hx_r)) * ring[0]
    k_y = mask * (hx_r * hz_r / (2.0 * hy_r)) * ring[1]
    k_z = mask * (hx_r * hy_r / (2.0 * hz_r)) * ring[2]
    layer_s = s_tab[3]
    hx_s = pick(s_tab[4], xs, ex)
    hz_s = pick(layer_s, zs, ez)
    keep = jnp.where(layer_s < count, 1.0, 0.0)
    scales = []
    for f in range(ey):
        denom = ys[f] * hz_s / (2.0 * hx_s) * s_tab[0]
        denom = denom + hx_s * hz_s / (2.0 * ys[f]) * s_tab[1]
        denom = denom + hx_s * ys[f] / (2.0 * hz_s) * s_tab[2]
        scales.append(keep / denom)
    scale = jnp.concatenate(scales, axis=0)
    rows_s = s_tab.shape[1]

    def schwarz(raw, target, make):
        spec_x = table_times(l_spec, raw)
        spec_x = jnp.concatenate(
            [spec_x[:, f * tile : (f + 3) * tile] for f in range(ey)], axis=0
        )
        spec = times(spec_x, r_spec) * scale
        fixed = times(spec, r_fix)
        fixed = jnp.concatenate(
            [fixed[f * rows_s : (f + 1) * rows_s] for f in range(ey)], axis=1
        )
        fixed = table_times(l_fix, fixed)
        fixed = inner_faces(fixed, in_low[:nx], in_high[:nx])
        target[8 : 8 + nx, tile : tile + lanes] = fixed
        return send_all(make)

    for copy in second:
        copy.wait_recv()
    down, up = 3 * nz, 6 * nz
    low_col = e_col[0, :, :down] + e_col[1, :, down:up]
    high_col = e_col[0, :, down:up] + e_col[2, :, :down]

    def cross_rows(value):
        width = value.shape[1]
        return (
            value
            + ring[9, :, :width] * pltpu.roll(value, rows - 1, 0)
            + ring[10, :, :width] * pltpu.roll(value, 1, 0)
        )

    cols = cross_rows(jnp.concatenate([low_col, high_col, jnp.zeros((rows, tile - up), F32)], axis=1))
    edge = jnp.concatenate(
        [
            e_row[0, 0:3] + e_row[1, 3:6],
            e_row[0, 3:6] + e_row[2, 0:3],
            jnp.zeros((2, wide), F32),
        ],
        axis=0,
    )
    edge = (
        edge
        + ring[11, :8] * pltpu.roll(edge, wide - nz, 1)
        + ring[12, :8] * pltpu.roll(edge, nz, 1)
    )
    ring_row = lax.broadcasted_iota(jnp.int32, (rows, wide), 0)
    at_low = (ring_row == 7) | (ring_row == 8)
    at_high = (ring_row == nx + 7) | (ring_row == nx + 8)
    gap = jnp.zeros((rows, tile - nz), F32)
    middle = jnp.zeros((rows, lanes - 2 * nz), F32)
    change = []
    for c in range(3):
        low = cols[:, c * nz : (c + 1) * nz]
        high = cols[:, down + c * nz : down + (c + 1) * nz]
        value = jnp.concatenate([gap, low, low, middle, high, high, gap], axis=1)
        value = jnp.where(at_low, edge[c : c + 1], value)
        value = jnp.where(at_high, edge[3 + c : 4 + c], value)
        change.append(value * inv_lumped * mask)
    adv = [known[c] - change[c][8 : 8 + nx, tile : tile + lanes] for c in range(3)]
    raw = e_draw[...] - (
        c_x * table_times(l_div, change[0])
        + c_y * unstacked(times(stacked(change[1], ey + 2), r_div_y), ey + 2)
        + c_z * unstacked(times(stacked(change[2], ey + 2), r_div_z), ey + 2)
    )
    third = schwarz(raw, e_fix1, block(e_fix1))
    for c in range(3):
        all_ref[c * nx : (c + 1) * nx, :] = adv[c]
    for copy in third:
        copy.wait_recv()
    press = cross(e_fix1[...]) * inv_mult
    by_y = stacked(press, ey + 2)
    raw = raw - (
        k_x * table_times(l_lap, press)
        + k_y * unstacked(times(by_y, r_lap_y), ey + 2)
        + k_z * unstacked(times(by_y, r_lap_z), ey + 2)
    )
    fourth = schwarz(raw, e_fix2, last_part)
    for copy in fourth:
        copy.wait_recv()
    press = press + cross(e_fix2[...]) * inv_mult
    all_ref[3 * nx :, :] = press[8 : 8 + nx, tile : tile + lanes]
    for copy in first + second + third + fourth:
        copy.wait_send()


def lay_out(nx, ny, nz, all_ref, adv_ref, press_ref, adv_buf, press_buf, sems):
    parts = 4
    some = nx // parts
    writes = []
    for part in range(parts):
        for c in range(3):
            at = c * nx + part * some
            own = all_ref[at : at + some, :]
            for y in range(ny):
                adv_buf[pl.ds(part * some * 3 * ny + c * ny + y, some, stride=3 * ny), :] = own[
                    :, y * nz : (y + 1) * nz
                ]
        at = 3 * nx + part * some
        own = all_ref[at : at + some, :]
        for y in range(ny):
            press_buf[pl.ds(part * some * ny + y, some, stride=ny), :] = own[
                :, y * nz : (y + 1) * nz
            ]
        for which, (buf, out, size) in enumerate(
            ((adv_buf, adv_ref, 3 * some * ny), (press_buf, press_ref, some * ny))
        ):
            span = pl.ds(part * size, size)
            copy = pltpu.make_async_copy(buf.at[span], out.at[span], sems.at[which, part])
            copy.start()
            writes.append(copy)
    for copy in writes:
        copy.wait()


def local(n_x, n_y, velocity, x_sizes, y_sizes, z_sizes, layer_counts):
    ex, ey, ez = x_sizes.shape[0], y_sizes.shape[0], z_sizes.shape[0]
    nx, ny, nz = 8 * ex, 8 * ey, 8 * ez
    tile = 8 * nz
    lanes = ny * nz
    rows, wide = nx + 16, lanes + 2 * tile
    vel = velocity.transpose(0, 2, 1, 3).reshape(3 * nx * ny, nz)
    consts = [jnp.asarray(c) for c in constants(ex, ey, ez)]
    vmem = pl.BlockSpec(memory_space=pltpu.VMEM)
    copies = 6 * 8 + 4
    scalars = (x_sizes, y_sizes, z_sizes, layer_counts)
    tables_in = (vel, *consts)
    both = pl.pallas_call(
        functools.partial(kernel, ex, ey, ez, n_x, n_y),
        out_shape=pltpu.VMEM((4 * nx, lanes), F32),
        in_specs=[pl.BlockSpec(memory_space=pltpu.HBM)] * (4 + len(tables_in)),
        out_specs=vmem,
        scratch_shapes=[pltpu.SMEM(a.shape, a.dtype) for a in scalars]
        + [pltpu.VMEM(a.shape, a.dtype) for a in tables_in]
        + [
            pltpu.VMEM((3, 8, wide), F32),
            pltpu.VMEM((2, rows, 128), F32),
            pltpu.VMEM((2, 8, wide), F32),
            pltpu.VMEM((3, rows, tile), F32),
            pltpu.VMEM((3, 8, wide), F32),
            pltpu.VMEM((rows, wide), F32),
            pltpu.VMEM((rows, wide), F32),
            pltpu.VMEM((rows, wide), F32),
            pltpu.SemaphoreType.DMA((copies,)),
            pltpu.SemaphoreType.DMA((copies,)),
            pltpu.SemaphoreType.DMA((4 + len(tables_in),)),
        ],
        compiler_params=pltpu.CompilerParams(collective_id=0, has_side_effects=True),
        name="sem_step",
    )(*scalars, *tables_in)
    adv, press = pl.pallas_call(
        functools.partial(lay_out, nx, ny, nz),
        out_shape=(
            jax.ShapeDtypeStruct((3 * nx * ny, nz), F32),
            jax.ShapeDtypeStruct((nx * ny, nz), F32),
        ),
        in_specs=[vmem],
        out_specs=(pl.BlockSpec(memory_space=pl.ANY),) * 2,
        scratch_shapes=[
            pltpu.VMEM((3 * nx * ny, nz), F32),
            pltpu.VMEM((nx * ny, nz), F32),
            pltpu.SemaphoreType.DMA((2, 4)),
        ],
        name="lay_out",
    )(pltpu.with_memory_space_constraint(both, pltpu.VMEM))
    advected = adv.reshape(nx, 3, ny, nz).transpose(0, 2, 1, 3)
    return advected, press.reshape(nx, ny, nz)


def solution(mesh):
    in_specs = (P("gx", "gy", None, None), P("gx"), P("gy"), P(), P("gx", "gy"))
    out_specs = (P("gx", "gy", None, None), P("gx", "gy", None))
    body = functools.partial(local, mesh.shape["gx"], mesh.shape["gy"])
    return jax.shard_map(body, mesh=mesh, in_specs=in_specs, out_specs=out_specs, check_vma=False)
```
